32 devices in a mesh: req: 4 (over y, core), mp: 8 (over z, x).
Axes of the slice: x: 2, y: 2, z: 4, core: 2. Of those that a mesh axis runs over, the one named last changes fastest.
Arguments:
- latents: bfloat16 [8, 4, 192, 2240], P('req', None, 'mp'), may hold values from -6 to 6
- w_qkv: bfloat16 [2240, 3360], P('mp'), may hold values from -0.125 to 0.125
- state_in: float32 [8, 10, 112, 112], P('req', None, 'mp'), may hold values from -384 to 384
- ksum_in: float32 [8, 10, 112], P('req'), may hold values from 64 to 1024
- frames_live: int32 [8], P('req'), may hold values from 1 to 4
- new_place: int32 [80], replicated, may hold values from 0 to 79, as said below
Outputs:
- attended: bfloat16 [8, 4, 192, 1120], P('req', None, 'mp')
- moved_state: float32 [80, 112, 112], P('req', 'mp')
- moved_ksum: float32 [80, 112], P('req')
The draws below stay inside these ranges and needn't reach their ends.
Inputs may be any that keep to these rules, and one draw needn't show every extreme that they name: new_place is a permutation; pair g of owner g // 20 goes to owner new_place[g] // 20; every owner receives 20 pairs, and from one owner at most 6 pairs go to one new owner, exactly 6 to some.
All inputs are finite; a program needn't handle non-finite values.
Results may differ from the reference program's by a relative error of at most 0.0075.
Values may be sent and summed in bfloat16 or wider, within the bound.
No kernel may reach another device: no remote copies, remote signals or barrier semaphores. Data moves between devices by JAX's collectives and lax.ppermute only.
A program may use at most 128 MiB of HBM per device.

```python
import math
import jax
import jax.numpy as jnp
from jax import lax

D = 2240
HEADS = 10
HEAD = 112
FRAMES = 4
STREAMS = 8
SPATIAL = 192
HW = 1120
UNITS = 20
N_REQ = 4


def draw_new_place(key, part):
    unit_count = UNITS
    owner_count = N_REQ
    key_one = jax.random.fold_in(key, 11)
    key_two = jax.random.fold_in(key, 12)
    priority = jax.random.permutation(key_one, owner_count).astype(jnp.int32)
    priority = priority.at[owner_count // 2].set(-2)
    priority = priority.at[1].set(-1)
    shuffle = jnp.argsort(priority).astype(jnp.int32)
    position = jnp.arange(unit_count, dtype=jnp.int32) % owner_count
    offsets = shuffle[position]
    offsets = offsets.at[unit_count - 1].set(shuffle[0])
    placing = jax.vmap(lambda single: jax.random.permutation(single, unit_count))(jax.random.split(key_two, owner_count))
    source = jnp.arange(owner_count, dtype=jnp.int32)[:, None]
    targets = (source + offsets[placing]) % owner_count
    return (targets * unit_count + placing).reshape(-1).astype(jnp.int32)


def with_ends(drawn, own_key, low, high):
    longest = drawn.shape.index(max(drawn.shape))
    spots = []
    for shift in (0, 1):
        where = [jax.random.randint(jax.random.fold_in(own_key, axis), (), 0, length) for axis, length in enumerate(drawn.shape)]
        where[longest] = (where[longest] + shift) % drawn.shape[longest]
        spots.append(tuple(where))
    return drawn.at[spots[0]].set(low).at[spots[1]].set(high)


def block_scale(key, shape, pieces, low, high):
    def one(axis_at, parts):
        steps = jax.random.uniform(jax.random.fold_in(jax.random.fold_in(key, 6), axis_at), (parts,), jnp.float32, low / len(pieces), high / len(pieces))
        return jnp.repeat(jnp.exp(steps), shape[axis_at] // parts).reshape((-1,) + (1,) * (len(shape) - axis_at - 1))

    level = one(*pieces[0])
    for cut in pieces[1:]:
        level = level * one(*cut)
    return level


def noise(rng, shape, scale, most, shards=(), kind=jnp.bfloat16):
    values = scale * jax.random.normal(rng, shape, jnp.float32)
    if shards:
        values = values * block_scale(rng, shape, shards, -0.22, 0.18)
    return jnp.clip(values, -most, most).astype(kind)


def setup_inputs(seed: int = 0) -> dict:
    key_list = jax.random.split(jax.random.key(seed), 7)
    return {
        "latents": noise(key_list[0], (STREAMS, FRAMES, SPATIAL, D), 1.0, 6.0, ((0, 4), (2, 8))),
        "w_qkv": noise(key_list[1], (D, 3 * HW), D ** -0.5, 0.125, ((0, 8),)),
        "state_in": noise(key_list[2], (STREAMS, HEADS, HEAD, HEAD), 64.0, 384.0, ((0, 4), (2, 8)), jnp.float32),
        "ksum_in": jnp.clip(jnp.exp(math.log(1024.0) - 2.7725887 * jax.random.uniform(key_list[3], (STREAMS, HEADS, HEAD), jnp.float32) ** block_scale(key_list[3], (STREAMS, HEADS, HEAD), ((0, 4),), -0.2, 0.2)), 64.0, 1024.0),
        "frames_live": with_ends(jax.random.randint(key_list[4], (STREAMS,), 1, FRAMES + 1), jax.random.fold_in(key_list[4], 1), 1, FRAMES).astype(jnp.int32),
        "new_place": draw_new_place(jax.random.fold_in(key_list[6], 71), 0),
    }


def feature_map(values):
    return jax.nn.elu(values) + 1.0


def reference(latents, w_qkv, state_in, ksum_in, frames_live, new_place):
    inner_width = HEADS * HEAD

    def one_stream(packed):
        block_rows, state_old, ksum_old, live_count = packed
        flat_rows = block_rows.reshape(-1, D)
        projected = jnp.dot(flat_rows, w_qkv, preferred_element_type=jnp.float32).astype(jnp.bfloat16)
        live_frames = (jnp.arange(FRAMES, dtype=jnp.int32) < live_count).astype(jnp.float32)
        live_rows = jnp.repeat(live_frames, SPATIAL)
        queried = feature_map(projected[:, :inner_width].astype(jnp.float32).reshape(-1, HEADS, HEAD))
        keyed = feature_map(projected[:, inner_width:2 * inner_width].astype(jnp.float32).reshape(-1, HEADS, HEAD))
        keyed = keyed * live_rows[:, None, None]
        values = projected[:, 2 * inner_width:].astype(jnp.float32).reshape(-1, HEADS, HEAD)
        state_new = state_old + jnp.einsum("thi,thj->hij", keyed, values, precision=lax.Precision.HIGHEST)
        ksum_new = ksum_old + jnp.sum(keyed, axis=0)
        numerator = jnp.einsum("thi,hij->thj", queried, state_new, precision=lax.Precision.HIGHEST)
        denominator = jnp.einsum("thi,hi->th", queried, ksum_new, precision=lax.Precision.HIGHEST)
        attended = (numerator / denominator[:, :, None]) * live_rows[:, None, None]
        return attended.astype(jnp.bfloat16).reshape(FRAMES, SPATIAL, inner_width), state_new, ksum_new

    attended, states, ksums = lax.map(one_stream, (latents, state_in, ksum_in, frames_live))
    flat_states = states.reshape(-1, HEAD, HEAD)
    flat_ksums = ksums.reshape(-1, HEAD)
    pair_count = new_place.shape[0]
    inverse = jnp.zeros((pair_count,), jnp.int32).at[new_place].set(jnp.arange(pair_count, dtype=jnp.int32))
    return attended, flat_states[inverse], flat_ksums[inverse]
```

```python
import functools

import jax
import jax.numpy as jnp
from jax import lax
from jax.experimental import pallas as pl
from jax.experimental.pallas import tpu as pltpu
from jax.sharding import Mesh
from jax.sharding import PartitionSpec as P

F32 = jnp.float32
BF16 = jnp.bfloat16
LANES = 128
VMEM = pl.BlockSpec(memory_space=pltpu.VMEM)
SMEM = pl.BlockSpec(memory_space=pltpu.SMEM)
SWAP = [(0, 1), (1, 0)]


def phi(u):
    return jnp.where(u > 0.0, u + 1.0, jnp.exp(jnp.minimum(u, 0.0)))


def whole_call(kernel, out_shape, smem_first, count, flops, moved):
    specs = [SMEM] * smem_first + [VMEM] * (count - smem_first)
    return pl.pallas_call(
        kernel,
        out_shape=out_shape,
        in_specs=specs,
        out_specs=jax.tree.map(lambda _: VMEM, out_shape),
        cost_estimate=pl.CostEstimate(flops=flops, bytes_accessed=moved, transcendentals=0),
        compiler_params=pltpu.CompilerParams(vmem_limit_bytes=56 * 1024 * 1024),
    )


def kv_kernel(streams, heads, size, rows, acc_ref, live_ref, group_ref, plain_ref, *outs):
    q_ref, chunks = outs[0], outs[1:]
    width = heads * size
    tokens = acc_ref.shape[0] // streams
    q_ref[...] = acc_ref[:, 2 * width :].astype(BF16)
    keys = acc_ref[:, :width].astype(BF16).astype(F32)
    keyed = (phi(keys) * live_ref[:, :1]).astype(BF16)
    values = acc_ref[:, width : 2 * width].astype(BF16)
    grouped = jnp.dot(keyed, group_ref[...], preferred_element_type=F32).astype(BF16)
    plain = jnp.dot(keyed, plain_ref[...], preferred_element_type=F32)
    spread = jnp.dot(values, plain_ref[...], preferred_element_type=F32)
    lane = lax.broadcasted_iota(jnp.int32, spread.shape, 1) % LANES
    spread = jnp.where(lane == size, 1.0, spread).astype(BF16)
    row = lax.broadcasted_iota(jnp.int32, (LANES, LANES), 0) % rows
    for s in range(streams):
        span = slice(s * tokens, (s + 1) * tokens)
        sums = jnp.sum(plain[span], axis=0, keepdims=True)
        for h in range(heads):
            cols = slice(h * LANES, (h + 1) * LANES)
            outer = lax.dot_general(
                grouped[span, cols],
                spread[span, cols],
                (((0,), (0,)), ((), ())),
                preferred_element_type=F32,
            )
            outer = jnp.where(row == rows - 1, sums[:, cols], outer).astype(BF16)
            for r, chunk in enumerate(chunks):
                chunk[s * heads + h] = outer[r * rows : (r + 1) * rows]


def read_kernel(streams, heads, size, y_ref, own_ref, other_ref, live_ref, group_ref, *refs):
    pieces, out_ref = refs[:-1], refs[-1]
    tokens = own_ref.shape[0] // streams
    first = y_ref[0] == 0
    own, other = own_ref[...], other_ref[...]
    halves = (jnp.where(first, own, other), jnp.where(first, other, own))
    for half, raw in enumerate(halves):
        queried = phi(raw.astype(F32)).astype(BF16)
        grouped = jnp.dot(queried, group_ref[...], preferred_element_type=F32).astype(BF16)
        for s in range(streams):
            span = slice(s * tokens, (s + 1) * tokens)
            live = live_ref[span, :1]
            for h in range(heads):
                pair = s * 2 * heads + half * heads + h
                state = jnp.concatenate([piece[pair] for piece in pieces], axis=0)
                top = jnp.dot(
                    grouped[span, h * LANES : (h + 1) * LANES],
                    state,
                    preferred_element_type=F32,
                )
                result = top[:, :size] / top[:, size : size + 1] * live
                col = (half * heads + h) * size
                out_ref[span, col : col + size] = result.astype(BF16)


def pick_kernel(share, size, rows, place_ref, all_ref, state_ref, ksum_ref):
    for u in range(state_ref.shape[0]):
        block = all_ref[place_ref[u]].astype(F32)
        state_ref[u] = block[:share, :size]
        ksum_ref[u : u + 1] = block[rows - 1 :, :size]


def body(n, latents, w_qkv, state_in, ksum_in, frames_live, new_place):
    streams, frames, spatial, model = latents.shape
    heads_all, size = ksum_in.shape[1:]
    heads = heads_all // 2
    share = state_in.shape[2]
    members = size // share
    rows = LANES // members
    width = heads * size
    depth = w_qkv.shape[0]
    units = streams * heads_all
    o, y, c = lax.axis_index("o"), lax.axis_index("y"), lax.axis_index("c")
    z, x = lax.axis_index("z"), lax.axis_index("x")
    m = z * 2 + x
    owners = lax.axis_size("o") * 4
    me = (o * 2 + y) * 2 + c

    def flat(cc, zz, xx):
        return (cc * n + zz) * 2 + xx

    def swap(axis, v):
        return lax.ppermute(v, axis, SWAP)

    def hop(k, v):
        pairs = [(i, i + 1) for i in range(k - 1, n - 1)]
        pairs += [(n + i, n + i - 1) for i in range(n - k, 0, -1)]
        return lax.ppermute(v, ("c", "z"), pairs)

    def across(k, v):
        pairs = [(flat(0, i, a), flat(0, i, 1 - a)) for i in range(k, n) for a in range(2)]
        pairs += [(flat(1, i, a), flat(1, i, 1 - a)) for i in range(0, n - k) for a in range(2)]
        return lax.ppermute(v, ("c", "z", "x"), pairs)

    def xor(k, v):
        return lax.ppermute(v, ("z", "x"), [(i, i ^ k) for i in range(members)])

    wq, wk, wv = (w_qkv[:, j * 2 * width : (j + 1) * 2 * width] for j in range(3))
    low = jnp.concatenate([v[:, :width] for v in (wk, wv, wq)], axis=1)
    high = jnp.concatenate([v[:, width:] for v in (wk, wv, wq)], axis=1)
    mine = jnp.where(y == 0, low, high)
    half = -(-depth // 16) * 8
    piece = jnp.where(c == 0, mine[:half], mine[depth - half :])

    Z = [None] * n
    X = [None] * n
    with jax.named_scope("z1"):
        Z[1] = hop(1, mine)
    with jax.named_scope("x0"):
        X[0] = swap("x", piece)
    own_tokens = latents.reshape(-1, model)
    with jax.named_scope("tok"):
        other_tokens = swap("y", own_tokens)
    live_own = (
        lax.broadcasted_iota(jnp.int32, (streams, frames), 1) < frames_live[:, None]
    ).astype(F32)
    live_other = swap("y", live_own)
    live = jnp.concatenate([live_own, live_other], axis=0)
    live = jnp.repeat(live.reshape(-1, 1), spatial, axis=0)
    live = jnp.broadcast_to(live, (live.shape[0], LANES))

    tokens = jnp.concatenate([own_tokens, other_tokens], axis=0)
    blocks = tokens.reshape(tokens.shape[0], members, depth).transpose(1, 0, 2)

    for k in range(1, n):
        if k > 1:
            with jax.named_scope(f"z{k}"):
                Z[k] = hop(k, Z[k - 1])
        with jax.named_scope(f"x{k}"):
            X[k] = across(k, Z[k])

    def block(line, col):
        return lax.dynamic_index_in_dim(blocks, (line % n) * 2 + col, 0, keepdims=False)

    def mul(a, b):
        return jnp.dot(a, b, preferred_element_type=F32)

    acc = mul(block(z, x), mine)
    there = block(z, 1 - x)
    rest = jnp.where(
        lax.broadcasted_iota(jnp.int32, (1, half), 1) < 2 * half - depth, 0, there[:, depth - half :]
    )
    x0_other = swap("c", X[0])
    lead, tail = jnp.where(c == 0, X[0], x0_other), jnp.where(c == 0, x0_other, X[0])
    acc = acc + mul(there[:, :half], lead) + mul(rest, tail)
    for k in range(1, n):
        near, far = z - k + 2 * k * c, z + k - 2 * k * c
        acc = acc + mul(block(near, x), Z[k]) + mul(block(far, x), swap("c", Z[k]))
        acc = acc + mul(block(near, 1 - x), X[k]) + mul(block(far, 1 - x), swap("c", X[k]))

    src = lax.broadcasted_iota(jnp.int32, (width, heads * LANES), 0)
    dst = lax.broadcasted_iota(jnp.int32, (width, heads * LANES), 1)
    same = (src // size) == (dst // LANES)
    spot, lane = src % size, dst % LANES
    plain = (same & (spot == lane)).astype(BF16)
    group = (
        same & (lane % rows < share) & (spot == ((lane // rows) ^ m) * share + lane % rows)
    ).astype(BF16)

    pairs = 2 * streams * heads
    chunk = jax.ShapeDtypeStruct((pairs, rows, LANES), BF16)
    q, *parts = whole_call(
        functools.partial(kv_kernel, 2 * streams, heads, size, rows),
        [jax.ShapeDtypeStruct((acc.shape[0], width), BF16)] + [chunk] * members,
        0,
        4,
        2_000_000_000,
        8_000_000,
    )(acc, live, group, plain)

    count = own_tokens.shape[0]
    with jax.named_scope("qy"):
        q_other = swap("y", q[count:])
    total = parts[0].astype(F32)
    for k in range(members - 1, 0, -1):
        with jax.named_scope(f"rs{k}"):
            total = total + xor(k, parts[k]).astype(F32)
    keep, give = total[: pairs // 2], total[pairs // 2 :]
    with jax.named_scope("sy"):
        got = swap("y", give.astype(BF16)).astype(F32)
    keep = keep.reshape(streams, 1, heads, rows, LANES)
    got = got.reshape(streams, 1, heads, rows, LANES)
    joined = jnp.where(
        y == 0, jnp.concatenate([keep, got], axis=1), jnp.concatenate([got, keep], axis=1)
    ).reshape(units, rows, LANES)

    old = state_in.reshape(units, share, size)
    ks = ksum_in.reshape(units, size)
    ks_rows = lax.dynamic_slice_in_dim(ks, m * share, share, 1)[:, :, None]
    old = jnp.concatenate(
        [old, ks_rows, jnp.zeros((units, share, LANES - size - 1), F32)], axis=2
    )
    ks_line = jnp.pad(ks, ((0, 0), (0, LANES - size)))[:, None]
    fill = jnp.zeros((units, rows - 1 - share, LANES), F32)
    old = jnp.concatenate([old, fill, ks_line], axis=1)
    new = (joined + old).astype(BF16)

    gathered = [new]
    for k in range(1, members):
        with jax.named_scope(f"ag{k}"):
            gathered.append(xor(k, new))

    every = new[None]
    bit = 1
    while bit < owners:
        step = [(i, i ^ bit) for i in range(owners)]
        with jax.named_scope(f"mv{bit}"):
            every = jnp.concatenate([every, lax.ppermute(every, ("o", "y", "c"), step)], axis=0)
        bit *= 2
    every = every.reshape(owners * units, rows, LANES)
    inverse = (
        jnp.zeros((owners * units,), jnp.int32)
        .at[new_place]
        .set(jnp.arange(owners * units, dtype=jnp.int32))
    )
    arrivals = lax.dynamic_slice_in_dim(inverse, me * units, units)
    place = ((arrivals // units) ^ me) * units + arrivals % units
    moved_state, moved_ksum = whole_call(
        functools.partial(pick_kernel, share, size, rows),
        [
            jax.ShapeDtypeStruct((units, share, size), F32),
            jax.ShapeDtypeStruct((units, size), F32),
        ],
        1,
        2,
        1_000_000,
        800_000,
    )(place, every)

    attended = whole_call(
        functools.partial(read_kernel, streams, heads, size),
        jax.ShapeDtypeStruct((count, 2 * width), BF16),
        1,
        5 + members,
        1_500_000_000,
        3_000_000,
    )(y.reshape(1).astype(jnp.int32), q[:count], q_other, live[:count], group, *gathered)
    return (
        attended.reshape(streams, frames, spatial, 2 * width),
        moved_state,
        moved_ksum,
    )


def solution(mesh):
    owners, members = mesh.shape["req"], mesh.shape["mp"]
    split = Mesh(
        mesh.devices.reshape(owners // 4, 2, 2, members // 2, 2), ("o", "y", "c", "z", "x")
    )
    req, mp = ("o", "y", "c"), ("z", "x")
    return jax.shard_map(
        functools.partial(body, members // 2),
        mesh=split,
        in_specs=(
            P(req, None, mp, None),
            P(mp, None),
            P(req, None, mp, None),
            P(req, None, None),
            P(req),
            P(),
        ),
        out_specs=(P(req, None, mp, None), P(req, mp, None), P(req, None)),
        check_vma=False,
    )
```

```python
import functools

import jax
import jax.numpy as jnp
from jax import lax
from jax.experimental import pallas as pl
from jax.experimental.pallas import tpu as pltpu
from jax.sharding import Mesh
from jax.sharding import PartitionSpec as P


F32 = jnp.float32
BF16 = jnp.bfloat16
LANES = 128
VMEM = pl.BlockSpec(memory_space=pltpu.VMEM)
SMEM = pl.BlockSpec(memory_space=pltpu.SMEM)
SWAP = [(0, 1), (1, 0)]


def phi(u):
    return jnp.where(u > 0.0, u + 1.0, jnp.exp(jnp.minimum(u, 0.0)))


def whole_call(kernel, out_shape, kinds, flops, moved, scratch=(), alias=None, smem=False):
    return pl.pallas_call(
        kernel,
        out_shape=out_shape,
        in_specs=[SMEM if kind == "s" else VMEM for kind in kinds],
        scratch_shapes=scratch,
        input_output_aliases=alias or {},
        out_specs=SMEM if smem else jax.tree.map(lambda _: VMEM, out_shape),
        cost_estimate=pl.CostEstimate(flops=flops, bytes_accessed=moved, transcendentals=0),
        compiler_params=pltpu.CompilerParams(vmem_limit_bytes=20 * 1024 * 1024),
    )


def prep_kernel(pos_ref, w_ref, mine_ref, piece_ref):
    depth, total = w_ref.shape
    half = piece_ref.shape[0]
    width = total // 6
    wide = mine_ref.shape[1]
    for turn in range(2):

        @pl.when(pos_ref[3] == turn)
        def _():
            for j, part in enumerate((1, 2, 0)):
                start = (2 * part + turn) * width
                mine_ref[:, j * width : (j + 1) * width] = w_ref[:, start : start + width]

    mine_ref[:, 3 * width :] = jnp.zeros((depth, wide - 3 * width), BF16)

    @pl.when(pos_ref[2] == 0)
    def _():
        piece_ref[...] = mine_ref[:half]

    @pl.when(pos_ref[2] == 1)
    def _():
        piece_ref[: depth - half] = mine_ref[half:]
        piece_ref[depth - half :] = jnp.zeros((2 * half - depth, wide), BF16)


def table_kernel(heads, rows, pos_ref, state_ref, ksum_ref, group_ref, plain_ref, old_ref):
    units, share, size = state_ref.shape
    m = pos_ref[4]
    src = lax.broadcasted_iota(jnp.int32, (size, LANES), 0)
    lane = lax.broadcasted_iota(jnp.int32, (size, LANES), 1)
    plain = jnp.where(src == lane, 1.0, 0.0).astype(BF16)
    spot = ((lane // rows) ^ m) * share + lane % rows
    group = jnp.where((src == spot) & (lane % rows < share), 1.0, 0.0).astype(BF16)
    group_ref[...] = jnp.zeros_like(group_ref)
    plain_ref[...] = jnp.zeros_like(plain_ref)
    for h in range(heads):
        group_ref[h * size : (h + 1) * size, h * LANES : (h + 1) * LANES] = group
        plain_ref[h * size : (h + 1) * size, h * LANES : (h + 1) * LANES] = plain
    row = lax.broadcasted_iota(jnp.int32, (rows, size), 0)
    col = lax.broadcasted_iota(jnp.int32, (rows, size), 1)
    chosen = jnp.where((col == m * share + row) & (row < share), 1.0, 0.0)
    ksum = ksum_ref[...]
    turned = lax.dot_general(
        chosen,
        ksum,
        (((1,), (1,)), ((), ())),
        precision=lax.Precision.HIGHEST,
        preferred_element_type=F32,
    )
    old_ref[...] = jnp.zeros_like(old_ref)
    for u in range(units):
        old_ref[u, :, size : size + 1] = turned[:, u : u + 1]
        old_ref[u, :share, :size] = state_ref[u]
        old_ref[u, rows - 1 :, :size] = ksum[u : u + 1]


def block_kernel(pos_ref, own_ref, other_ref, out_ref):
    members, both, wide = out_ref.shape
    count = both // 2
    depth = own_ref.shape[1] // members
    for b in range(members):
        out_ref[b, :count, :depth] = own_ref[:, b * depth : (b + 1) * depth]
        out_ref[b, count:, :depth] = other_ref[:, b * depth : (b + 1) * depth]
        if wide > depth:
            out_ref[b, :, depth:] = jnp.zeros((both, wide - depth), BF16)


def hops(n, pos_ref, k, cross):
    z, x, c = pos_ref[0], pos_ref[1], pos_ref[2]
    col = 1 - x if cross else x
    first = 2 if cross and k == 1 else k
    up, down = lax.rem(z - k + n, n), lax.rem(z + k, n)
    if 2 * first > n - 1:
        return (jnp.where(z >= first, up, down) * 2 + col,)
    return (jnp.where(c == 0, up, down) * 2 + col, jnp.where(c == 0, down, up) * 2 + col)


def add_products(n, plan, pos_ref, blocks_ref, refs, tile):
    total = None
    refs = list(refs)
    for kind, k in plan:
        if kind == "own":
            terms = [(pos_ref[0] * 2 + pos_ref[1], refs.pop(0)[:, tile])]
        elif kind in ("beside", "corner"):
            here, there = refs.pop(0)[:, tile], refs.pop(0)[:, tile]
            first = pos_ref[2] == 0
            line = pos_ref[0]
            if kind == "corner":
                line = jnp.where(line <= 1, 0, n - 1)
            both = jnp.concatenate(
                [jnp.where(first, here, there), jnp.where(first, there, here)], axis=0
            )
            terms = [(line * 2 + 1 - pos_ref[1], both)]
        else:
            here, there = refs.pop(0)[:, tile], refs.pop(0)[:, tile]
            ids = hops(n, pos_ref, k, kind == "across")
            terms = [(ids[0], here + there)] if len(ids) == 1 else list(zip(ids, (here, there)))
        for index, weight in terms:
            lhs = blocks_ref[index, :, : weight.shape[0]]
            term = jnp.dot(lhs, weight, preferred_element_type=F32)
            total = term if total is None else total + term
    return total


def mul_kernel(n, plan, fresh, pos_ref, blocks_ref, *refs):
    acc_ref = refs[-1]
    given = refs[:-1] if fresh else refs[1:-1]
    wide = acc_ref.shape[1]
    step = 256 if wide % 256 == 0 else LANES

    @pl.loop(0, wide // step)
    def _(t):
        tile = pl.ds(pl.multiple_of(t * step, step), step)
        term = add_products(n, plan, pos_ref, blocks_ref, given, tile)
        acc_ref[:, tile] = term if fresh else refs[0][:, tile] + term


def kv_kernel(n, plan, streams, frames, heads, size, rows, pos_ref, near_ref, far_ref, *refs):
    blocks_ref, old_ref, refs = refs[0], refs[1], refs[2:]
    given, refs = refs[: 2 * len(plan)], refs[2 * len(plan) :]
    group_ref, plain_ref, mine_ref, give_ref = refs[:4]
    chunks, acc_ref = refs[4:-1], refs[-1]
    wide = acc_ref.shape[1]
    step = 256 if wide % 256 == 0 else LANES

    @pl.loop(0, wide // step)
    def _(t):
        tile = pl.ds(pl.multiple_of(t * step, step), step)
        acc_ref[:, tile] = old_ref[:, tile] + add_products(
            n, plan, pos_ref, blocks_ref, given, tile
        )

    width = heads * size
    count = acc_ref.shape[0] // 2
    tokens = count // streams
    asked = acc_ref[:, 2 * width : 3 * width].astype(BF16)
    mine_ref[...] = asked[:count]
    give_ref[...] = asked[count:]
    frame = lax.broadcasted_iota(jnp.int32, (tokens, width), 0) // (tokens // frames)
    masks = [frame < ref[s] for ref in (near_ref, far_ref) for s in range(streams)]
    live = jnp.concatenate([jnp.where(mask, 1.0, 0.0) for mask in masks], axis=0)
    keys = acc_ref[:, :width].astype(BF16).astype(F32)
    keyed = (phi(keys) * live).astype(BF16)
    values = acc_ref[:, width : 2 * width].astype(BF16)
    grouped = jnp.dot(keyed, group_ref[...], preferred_element_type=F32).astype(BF16)
    plain = jnp.dot(keyed, plain_ref[...], preferred_element_type=F32)
    spread = jnp.dot(values, plain_ref[...], preferred_element_type=F32)
    lane = lax.broadcasted_iota(jnp.int32, spread.shape, 1) % LANES
    spread = jnp.where(lane == size, 1.0, spread).astype(BF16)
    row = lax.broadcasted_iota(jnp.int32, (LANES, LANES), 0) % rows
    for s in range(2 * streams):
        span = slice(s * tokens, (s + 1) * tokens)
        sums = jnp.sum(plain[span], axis=0, keepdims=True)
        for h in range(heads):
            cols = slice(h * LANES, (h + 1) * LANES)
            outer = lax.dot_general(
                grouped[span, cols],
                spread[span, cols],
                (((0,), (0,)), ((), ())),
                preferred_element_type=F32,
            )
            outer = jnp.where(row == rows - 1, sums[:, cols], outer).astype(BF16)
            for r, chunk in enumerate(chunks):
                chunk[s * heads + h] = outer[r * rows : (r + 1) * rows]


def sum_kernel(*refs):
    parts, keep_ref, give_ref = refs[1:-2], refs[-2], refs[-1]
    half = keep_ref.shape[0]
    for lo, out in ((0, keep_ref), (half, give_ref)):
        total = parts[0][lo : lo + half].astype(F32)
        for part in parts[1:]:
            total = total + part[lo : lo + half].astype(F32)
        out[...] = total.astype(out.dtype)


def join_kernel(heads, pos_ref, keep_ref, got_ref, old_ref, new_ref):
    first = pos_ref[3] == 0
    for s in range(keep_ref.shape[0] // heads):
        keep = keep_ref[s * heads : (s + 1) * heads]
        got = got_ref[s * heads : (s + 1) * heads].astype(F32)
        at = 2 * s * heads
        low = jnp.where(first, keep, got) + old_ref[at : at + heads]
        high = jnp.where(first, got, keep) + old_ref[at + heads : at + 2 * heads]
        new_ref[at : at + heads] = low.astype(BF16)
        new_ref[at + heads : at + 2 * heads] = high.astype(BF16)


def query_kernel(pos_ref, raw_ref, group_ref, out_ref):
    queried = phi(raw_ref[...].astype(F32)).astype(BF16)
    out_ref[...] = jnp.dot(queried, group_ref[...], preferred_element_type=F32).astype(BF16)


def read_kernel(streams, frames, heads, size, pos_ref, near_ref, own_ref, other_ref, *refs):
    pieces, out_ref = refs[:-1], refs[-1]
    tokens = own_ref.shape[0] // streams
    first = pos_ref[3] == 0
    frame = lax.broadcasted_iota(jnp.int32, (tokens, 1), 0) // (tokens // frames)
    own, other = own_ref[...], other_ref[...]
    halves = (jnp.where(first, own, other), jnp.where(first, other, own))
    for s in range(streams):
        span = slice(s * tokens, (s + 1) * tokens)
        live = jnp.where(frame < near_ref[s], 1.0, 0.0)
        for half, grouped in enumerate(halves):
            for h in range(heads):
                pair = s * 2 * heads + half * heads + h
                state = jnp.concatenate([piece[pair] for piece in pieces], axis=0)
                top = jnp.dot(
                    grouped[span, h * LANES : (h + 1) * LANES],
                    state,
                    preferred_element_type=F32,
                )
                result = top[:, :size] / top[:, size : size + 1] * live
                col = (half * heads + h) * size
                out_ref[span, col : col + size] = result.astype(BF16)


def place_kernel(units, pos_ref, new_ref, place_ref):
    me = pos_ref[5]

    @pl.loop(0, new_ref.shape[0])
    def _(g):
        spot = new_ref[g]

        @pl.when(spot // units == me)
        def _():
            place_ref[spot % units] = ((g // units) ^ me) * units + g % units


def pick_kernel(share, size, rows, spots, place_ref, *refs):
    given, (state_ref, ksum_ref, all_ref) = refs[:-3], refs[-3:]
    units = state_ref.shape[0]
    for spot, ref in zip(spots, given):
        all_ref[spot * units : (spot + 1) * units] = ref[...]
    for u in range(units):
        block = all_ref[place_ref[u]].astype(F32)
        state_ref[u] = block[:share, :size]
        ksum_ref[u : u + 1] = block[rows - 1 :, :size]


def body(n, *given):
    return layer(n, *given)


def layer(n, latents, w_qkv, state_in, ksum_in, frames_live, new_place):
    streams, frames, spatial, model = latents.shape
    heads_all, size = ksum_in.shape[1:]
    heads = heads_all // 2
    share = state_in.shape[2]
    members = size // share
    rows = LANES // members
    width = heads * size
    depth = w_qkv.shape[0]
    units = streams * heads_all
    o, y, c = lax.axis_index("o"), lax.axis_index("y"), lax.axis_index("c")
    z, x = lax.axis_index("z"), lax.axis_index("x")
    m = z * 2 + x
    owners = lax.axis_size("o") * 4
    me = (o * 2 + y) * 2 + c

    def flat(cc, zz, xx):
        return (cc * n + zz) * 2 + xx

    def swap(axis, v):
        return lax.ppermute(v, axis, SWAP)

    def hop(k, v):
        pairs = [(i, i + 1) for i in range(k - 1, n - 1)]
        pairs += [(n + i, n + i - 1) for i in range(n - k, 0, -1)]
        return lax.ppermute(v, ("c", "z"), pairs)

    def across(k, v):
        first = 2 if k == 1 else k
        pairs = [(flat(0, i, a), flat(0, i, 1 - a)) for i in range(first, n) for a in range(2)]
        pairs += [(flat(1, i, a), flat(1, i, 1 - a)) for i in range(n - first) for a in range(2)]
        return lax.ppermute(v, ("c", "z", "x"), pairs)

    def xor(k, v):
        return lax.ppermute(v, ("z", "x"), [(i, i ^ k) for i in range(members)])

    def near_end(v):
        pairs = [(flat(i, 0, a), flat(i, 1, a)) for i in range(2) for a in range(2)]
        pairs += [(flat(i, n - 1, a), flat(i, n - 2, a)) for i in range(2) for a in range(2)]
        return lax.ppermute(v, ("c", "z", "x"), pairs)

    pos = jnp.stack([z, x, c, y, m, me]).astype(jnp.int32)
    wide = -(-3 * width // LANES) * LANES
    half = -(-depth // 32) * 16
    mine, piece = whole_call(
        prep_kernel,
        [jax.ShapeDtypeStruct((depth, wide), BF16), jax.ShapeDtypeStruct((half, wide), BF16)],
        "sv",
        0,
        4_000_000,
    )(pos, w_qkv)

    own_tokens = latents.reshape(-1, model)
    count = own_tokens.shape[0]
    Z, X, ZC, XC = ([None] * n for _ in range(4))
    Z[1] = hop(1, mine)
    X[0] = swap("x", piece)
    other_tokens = swap("y", own_tokens)
    far_live = swap("y", frames_live)
    for k in range(1, n):
        if k > 1:
            Z[k] = hop(k, Z[k - 1])
        X[k] = across(k, Z[k])
        ZC[k] = swap("c", Z[k])
    Y = near_end(X[0])
    YC = swap("c", Y)
    for k in range(n):
        XC[k] = swap("c", X[k])

    group, plain, old = whole_call(
        functools.partial(table_kernel, heads, rows),
        [
            jax.ShapeDtypeStruct((width, heads * LANES), BF16),
            jax.ShapeDtypeStruct((width, heads * LANES), BF16),
            jax.ShapeDtypeStruct((units, rows, LANES), F32),
        ],
        "svv",
        0,
        2_000_000,
    )(pos, state_in.reshape(units, share, size), ksum_in.reshape(units, size))
    blocks = whole_call(
        block_kernel,
        jax.ShapeDtypeStruct((members, 2 * count, 2 * half), BF16),
        "svv",
        0,
        4_000_000,
    )(pos, own_tokens, other_tokens)

    def multiply(plan, acc, *given):
        first = [] if acc is None else [acc]
        return whole_call(
            functools.partial(mul_kernel, n, plan, acc is None),
            jax.ShapeDtypeStruct((2 * count, wide), F32),
            "sv" + "v" * (len(first) + len(given)),
            2_000_000_000,
            8_000_000,
            alias={2: 0} if first else None,
        )(pos, blocks, *first, *given)

    acc = multiply([("own", 0), ("beside", 0), ("along", 1)], None, mine, X[0], XC[0], Z[1], ZC[1])
    for k in range(2, n):
        plan = [("across", k - 1), ("along", k)]
        given = [X[k - 1], XC[k - 1], Z[k], ZC[k]]
        if k == 2:
            plan, given = plan + [("corner", 0)], given + [Y, YC]
        acc = multiply(plan, acc, *given)

    pairs = 2 * streams * heads
    chunk = jax.ShapeDtypeStruct((pairs, rows, LANES), BF16)
    asked = jax.ShapeDtypeStruct((count, width), BF16)
    q, q_give, *parts = whole_call(
        functools.partial(
            kv_kernel, n, [("across", n - 1)], streams, frames, heads, size, rows
        ),
        [asked, asked] + [chunk] * members,
        "sssvvvvvv",
        2_000_000_000,
        8_000_000,
        scratch=[pltpu.VMEM((2 * count, wide), F32)],
    )(pos, frames_live, far_live, blocks, acc, X[n - 1], XC[n - 1], group, plain)

    for k in range(members - 1, 0, -1):
        parts[k] = xor(k, parts[k])
    q_other = swap("y", q_give)

    def ask(raw):
        return whole_call(
            query_kernel,
            jax.ShapeDtypeStruct((count, heads * LANES), BF16),
            "svv",
            140_000_000,
            1_500_000,
        )(pos, raw, group)

    q = ask(q)
    keep, give = whole_call(
        sum_kernel,
        [
            jax.ShapeDtypeStruct((pairs // 2, rows, LANES), F32),
            jax.ShapeDtypeStruct((pairs // 2, rows, LANES), BF16),
        ],
        "s" + "v" * members,
        0,
        1_000_000,
    )(pos, *parts)
    got = swap("y", give)
    new = whole_call(
        functools.partial(join_kernel, heads),
        jax.ShapeDtypeStruct((units, rows, LANES), BF16),
        "svvv",
        0,
        500_000,
    )(pos, keep, got, old)

    gathered = [new] + [xor(k, new) for k in range(1, members)]
    q_other = ask(q_other)

    every, spots, bit = [new], [0], owners // 2
    while bit:
        step = [(i, i ^ bit) for i in range(owners)]
        for i in range(len(every)):
            moved = lax.ppermute(every[i], ("o", "y", "c"), step)
            every.append(moved)
            spots.append(spots[i] ^ bit)
        bit //= 2
    place = whole_call(
        functools.partial(place_kernel, units),
        jax.ShapeDtypeStruct((units,), jnp.int32),
        "ss",
        0,
        1_000,
        smem=True,
    )(pos, new_place)
    moved_state, moved_ksum = whole_call(
        functools.partial(pick_kernel, share, size, rows, spots),
        [
            jax.ShapeDtypeStruct((units, share, size), F32),
            jax.ShapeDtypeStruct((units, size), F32),
        ],
        "s" + "v" * owners,
        1_000_000,
        800_000,
        scratch=[pltpu.VMEM((owners * units, rows, LANES), BF16)],
    )(place, *every)

    attended = whole_call(
        functools.partial(read_kernel, streams, frames, heads, size),
        jax.ShapeDtypeStruct((count, 2 * width), BF16),
        "ssvv" + "v" * members,
        1_500_000_000,
        3_000_000,
    )(pos, frames_live, q, q_other, *gathered)
    return (
        attended.reshape(streams, frames, spatial, 2 * width),
        moved_state,
        moved_ksum,
    )


def solution(mesh):
    owners, members = mesh.shape["req"], mesh.shape["mp"]
    split = Mesh(
        mesh.devices.reshape(owners // 4, 2, 2, members // 2, 2), ("o", "y", "c", "z", "x")
    )
    req, mp = ("o", "y", "c"), ("z", "x")
    return jax.shard_map(
        functools.partial(body, members // 2),
        mesh=split,
        in_specs=(
            P(req, None, mp, None),
            P(mp, None),
            P(req, None, mp, None),
            P(req, None, None),
            P(req),
            P(),
        ),
        out_specs=(P(req, None, mp, None), P(req, mp, None), P(req, None)),
        check_vma=False,
    )
```

```python
import functools

import jax
import jax.numpy as jnp
from jax import lax
from jax.experimental import pallas as pl
from jax.experimental.pallas import tpu as pltpu
from jax.sharding import Mesh
from jax.sharding import PartitionSpec as P


F32 = jnp.float32
BF16 = jnp.bfloat16
LANES = 128
VMEM = pl.BlockSpec(memory_space=pltpu.VMEM)
SMEM = pl.BlockSpec(memory_space=pltpu.SMEM)
SPECS = {"s": SMEM, "v": VMEM, "h": pl.BlockSpec(memory_space=pltpu.HBM)}
SWAP = [(0, 1), (1, 0)]


def swap_plan():
    spots = [(c, z, x) for c in range(2) for z in range(4) for x in range(2)]
    partners, sent, held = [], [], [{(c, z, x): (z, x) for c, z, x in spots}]
    for k in range(1, 5):
        pair, send = {}, {}
        for c, z, x in spots:
            end = z in (0, 3)
            line = (c, z ^ 1, x)
            side = (c, z, 1 - x)
            middle = side if end else (c, 3 - z, x)
            straight = c == (k + 1) % 2
            if k < 3:
                pair[c, z, x] = line if straight else middle
            else:
                pair[c, z, x] = line if straight == (k == 3) else side
            send[c, z, x] = k - 1
            if k == 4:
                pair[c, z, x] = side if c == 0 else line
            if not end and ((k == 3 and c == 1) or (k == 4 and c == 0)):
                send[c, z, x] = k - 2
        partners.append(pair)
        sent.append(send)
        held.append({spot: held[send[pair[spot]]][pair[spot]] for spot in spots})
    return partners, sent, held


def phi(u):
    return jnp.where(u > 0.0, u + 1.0, jnp.exp(jnp.minimum(u, 0.0)))


def whole_call(kernel, out_shape, kinds, flops, moved, scratch=(), alias=None, smem=False):
    return pl.pallas_call(
        kernel,
        out_shape=out_shape,
        in_specs=[SPECS[kind] for kind in kinds],
        scratch_shapes=scratch,
        input_output_aliases=alias or {},
        out_specs=SMEM if smem else jax.tree.map(lambda _: VMEM, out_shape),
        cost_estimate=pl.CostEstimate(flops=flops, bytes_accessed=moved, transcendentals=0),
        compiler_params=pltpu.CompilerParams(vmem_limit_bytes=20 * 1024 * 1024),
    )


def prep_kernel(kinds, pos_ref, w_hbm, out_ref, w_ref, sems):
    depth, total = w_hbm.shape
    width = total // 6
    cuts = sems.shape[0]
    edges = [depth * i // cuts // 8 * 8 for i in range(cuts)] + [depth]
    spans = list(zip(edges, edges[1:]))
    low = min(kinds) * 2 * width // LANES * LANES
    high = min(-(-(max(kinds) + 1) * 2 * width // LANES) * LANES, total)
    copies = []
    for i, (lo, hi) in enumerate(spans):
        if high == total:
            low, source, target = 0, w_hbm.at[lo:hi], w_ref.at[lo:hi]
        else:
            source, target = w_hbm.at[lo:hi, low:high], w_ref.at[lo:hi, : high - low]
        copies.append(pltpu.make_async_copy(source, target, sems.at[i]))
    for copy in copies:
        copy.start()
    used = len(kinds) * width
    if used < out_ref.shape[1]:
        out_ref[:, used:] = jnp.zeros((depth, out_ref.shape[1] - used), BF16)
    for copy, (lo, hi) in zip(copies, spans):
        copy.wait()
        for turn in range(2):

            @pl.when(pos_ref[3] == turn)
            def _():
                for j, kind in enumerate(kinds):
                    start = (2 * kind + turn) * width - low
                    out_ref[lo:hi, j * width : (j + 1) * width] = w_ref[
                        lo:hi, start : start + width
                    ]


def choose_kernel(core, pos_ref, early_ref, late_ref, out_ref):
    early = (pos_ref[6] == 1) & (pos_ref[2] == core)

    @pl.when(early)
    def _():
        out_ref[...] = early_ref[...]

    @pl.when(jnp.logical_not(early))
    def _():
        out_ref[...] = late_ref[...]


def table_kernel(heads, rows, pos_ref, state_ref, ksum_ref, group_ref, plain_ref, old_ref):
    units, share, size = state_ref.shape
    m = pos_ref[4]
    src = lax.broadcasted_iota(jnp.int32, (size, LANES), 0)
    lane = lax.broadcasted_iota(jnp.int32, (size, LANES), 1)
    plain = jnp.where(src == lane, 1.0, 0.0).astype(BF16)
    spot = ((lane // rows) ^ m) * share + lane % rows
    group = jnp.where((src == spot) & (lane % rows < share), 1.0, 0.0).astype(BF16)
    group_ref[...] = jnp.zeros_like(group_ref)
    plain_ref[...] = jnp.zeros_like(plain_ref)
    for h in range(heads):
        group_ref[h * size : (h + 1) * size, h * LANES : (h + 1) * LANES] = group
        plain_ref[h * size : (h + 1) * size, h * LANES : (h + 1) * LANES] = plain
    row = lax.broadcasted_iota(jnp.int32, (rows, size), 0)
    col = lax.broadcasted_iota(jnp.int32, (rows, size), 1)
    chosen = jnp.where((col == m * share + row) & (row < share), 1.0, 0.0)
    ksum = ksum_ref[...]
    turned = lax.dot_general(
        chosen,
        ksum,
        (((1,), (1,)), ((), ())),
        precision=lax.Precision.HIGHEST,
        preferred_element_type=F32,
    )
    old_ref[...] = jnp.zeros_like(old_ref)
    for u in range(units):
        old_ref[u, :, size : size + 1] = turned[:, u : u + 1]
        old_ref[u, :share, :size] = state_ref[u]
        old_ref[u, rows - 1 :, :size] = ksum[u : u + 1]


def block_kernel(pos_ref, own_ref, other_ref, out_ref):
    members, both, _ = out_ref.shape
    count = both // 2
    depth = own_ref.shape[1] // members
    for b in range(members):
        out_ref[b, :count, :depth] = own_ref[:, b * depth : (b + 1) * depth]
        out_ref[b, count:, :depth] = other_ref[:, b * depth : (b + 1) * depth]


def add_products(slots, pos_ref, blocks_ref, refs, tile):
    terms = []
    if slots == ("core",):
        first = pos_ref[2] == 0
        weight = jnp.where(first, refs[0][:, tile], refs[1][:, tile])
        terms = [(jnp.where(first, pos_ref[14], pos_ref[15]), weight)]
    elif slots == ("all",):
        terms = [(b, refs[0][b, :, tile]) for b in range(refs[0].shape[0])]
    else:
        terms = [(pos_ref[slot], ref[:, tile]) for slot, ref in zip(slots, refs)]
    total = None
    for index, weight in terms:
        term = jnp.dot(blocks_ref[index], weight, preferred_element_type=F32)
        total = term if total is None else total + term
    return total


def column_step(wide):
    return next(step for step in (384, 256, LANES) if wide % step == 0)


def mul_kernel(slots, fresh, pos_ref, blocks_ref, *refs):
    acc_ref = refs[-1]
    given = refs[:-1] if fresh else refs[1:-1]
    step = column_step(acc_ref.shape[1])

    @pl.loop(0, acc_ref.shape[1] // step)
    def _(t):
        tile = pl.ds(pl.multiple_of(t * step, step), step)
        term = add_products(slots, pos_ref, blocks_ref, given, tile)
        acc_ref[:, tile] = term if fresh else refs[0][:, tile] + term


def ask_kernel(slots, width, pos_ref, blocks_ref, old_ref, group_ref, *refs):
    given, (mine_ref, give_ref, acc_ref) = refs[:-3], refs[-3:]
    step = column_step(acc_ref.shape[1])

    @pl.loop(0, acc_ref.shape[1] // step)
    def _(t):
        tile = pl.ds(pl.multiple_of(t * step, step), step)
        acc_ref[:, tile] = old_ref[:, tile] + add_products(
            slots, pos_ref, blocks_ref, given, tile
        )

    count = acc_ref.shape[0] // 2
    give_ref[...] = acc_ref[count:, :width].astype(BF16)
    raw = acc_ref[:count, :width].astype(BF16)
    queried = phi(raw.astype(F32)).astype(BF16)
    mine_ref[...] = jnp.dot(queried, group_ref[...], preferred_element_type=F32).astype(BF16)


def kv_kernel(slots, streams, frames, heads, size, rows, pos_ref, near_ref, far_ref, *refs):
    blocks_ref, old_ref, refs = refs[0], refs[1], refs[2:]
    count = 2 if slots == ("core",) else 1
    given, refs = refs[:count], refs[count:]
    group_ref, plain_ref = refs[:2]
    chunks, acc_ref = refs[2:-1], refs[-1]
    step = column_step(acc_ref.shape[1])

    @pl.loop(0, acc_ref.shape[1] // step)
    def _(t):
        tile = pl.ds(pl.multiple_of(t * step, step), step)
        acc_ref[:, tile] = old_ref[:, tile] + add_products(
            slots, pos_ref, blocks_ref, given, tile
        )

    width = heads * size
    count = acc_ref.shape[0] // 2
    tokens = count // streams
    frame = lax.broadcasted_iota(jnp.int32, (tokens, width), 0) // (tokens // frames)
    masks = [frame < ref[s] for ref in (near_ref, far_ref) for s in range(streams)]
    live = jnp.concatenate([jnp.where(mask, 1.0, 0.0) for mask in masks], axis=0)
    keys = acc_ref[:, :width].astype(BF16).astype(F32)
    keyed = (phi(keys) * live).astype(BF16)
    values = acc_ref[:, width : 2 * width].astype(BF16)
    grouped = jnp.dot(keyed, group_ref[...], preferred_element_type=F32).astype(BF16)
    plain = jnp.dot(keyed, plain_ref[...], preferred_element_type=F32)
    spread = jnp.dot(values, plain_ref[...], preferred_element_type=F32)
    lane = lax.broadcasted_iota(jnp.int32, spread.shape, 1) % LANES
    spread = jnp.where(lane == size, 1.0, spread).astype(BF16)
    row = lax.broadcasted_iota(jnp.int32, (LANES, LANES), 0) % rows
    for s in range(2 * streams):
        span = slice(s * tokens, (s + 1) * tokens)
        sums = jnp.sum(plain[span], axis=0, keepdims=True)
        for h in range(heads):
            cols = slice(h * LANES, (h + 1) * LANES)
            outer = lax.dot_general(
                grouped[span, cols],
                spread[span, cols],
                (((0,), (0,)), ((), ())),
                preferred_element_type=F32,
            )
            outer = jnp.where(row == rows - 1, sums[:, cols], outer).astype(BF16)
            for r, chunk in enumerate(chunks):
                chunk[s * heads + h] = outer[r * rows : (r + 1) * rows]


def sum_kernel(*refs):
    parts, keep_ref, give_ref = refs[1:-2], refs[-2], refs[-1]
    half = keep_ref.shape[0]
    for lo, out in ((0, keep_ref), (half, give_ref)):
        total = parts[0][lo : lo + half].astype(F32)
        for part in parts[1:]:
            total = total + part[lo : lo + half].astype(F32)
        out[...] = total.astype(out.dtype)


def join_kernel(heads, pos_ref, keep_ref, got_ref, old_ref, new_ref):
    first = pos_ref[3] == 0
    for s in range(keep_ref.shape[0] // heads):
        keep = keep_ref[s * heads : (s + 1) * heads]
        got = got_ref[s * heads : (s + 1) * heads].astype(F32)
        at = 2 * s * heads
        low = jnp.where(first, keep, got) + old_ref[at : at + heads]
        high = jnp.where(first, got, keep) + old_ref[at + heads : at + 2 * heads]
        new_ref[at : at + heads] = low.astype(BF16)
        new_ref[at + heads : at + 2 * heads] = high.astype(BF16)


def query_kernel(pos_ref, raw_ref, group_ref, out_ref):
    queried = phi(raw_ref[...].astype(F32)).astype(BF16)
    out_ref[...] = jnp.dot(queried, group_ref[...], preferred_element_type=F32).astype(BF16)


def read_kernel(streams, frames, heads, size, pos_ref, near_ref, own_ref, other_ref, *refs):
    pieces, out_ref = refs[:-1], refs[-1]
    tokens = own_ref.shape[0] // streams
    first = pos_ref[3] == 0
    frame = lax.broadcasted_iota(jnp.int32, (tokens, 1), 0) // (tokens // frames)
    own, other = own_ref[...], other_ref[...]
    halves = (jnp.where(first, own, other), jnp.where(first, other, own))
    for s in range(streams):
        span = slice(s * tokens, (s + 1) * tokens)
        live = jnp.where(frame < near_ref[s], 1.0, 0.0)
        for half, grouped in enumerate(halves):
            for h in range(heads):
                pair = s * 2 * heads + half * heads + h
                state = jnp.concatenate([piece[pair] for piece in pieces], axis=0)
                top = jnp.dot(
                    grouped[span, h * LANES : (h + 1) * LANES],
                    state,
                    preferred_element_type=F32,
                )
                result = top[:, :size] / top[:, size : size + 1] * live
                col = (half * heads + h) * size
                out_ref[span, col : col + size] = result.astype(BF16)


def place_kernel(units, pos_ref, new_ref, place_ref):
    me = pos_ref[5]

    @pl.loop(0, new_ref.shape[0])
    def _(g):
        spot = new_ref[g]

        @pl.when(spot // units == me)
        def _():
            place_ref[spot % units] = ((g // units) ^ me) * units + g % units


def pick_kernel(share, size, rows, spots, place_ref, *refs):
    given, (state_ref, ksum_ref, all_ref) = refs[:-3], refs[-3:]
    units = state_ref.shape[0]
    for spot, ref in zip(spots, given):
        all_ref[spot * units : (spot + 1) * units] = ref[...]
    for u in range(units):
        block = all_ref[place_ref[u]].astype(F32)
        state_ref[u] = block[:share, :size]
        ksum_ref[u : u + 1] = block[rows - 1 :, :size]


def body(n, *given):
    return layer(n, *given)


def layer(n, latents, w_qkv, state_in, ksum_in, frames_live, new_place):
    streams, frames, spatial, model = latents.shape
    heads_all, size = ksum_in.shape[1:]
    heads = heads_all // 2
    share = state_in.shape[2]
    members = size // share
    rows = LANES // members
    width = heads * size
    depth = w_qkv.shape[0]
    units = streams * heads_all
    o, y, c = lax.axis_index("o"), lax.axis_index("y"), lax.axis_index("c")
    z, x = lax.axis_index("z"), lax.axis_index("x")
    m = z * 2 + x
    owners = lax.axis_size("o") * 4
    me = (o * 2 + y) * 2 + c

    def swap(axis, v):
        return lax.ppermute(v, axis, SWAP)

    def xor(k, v):
        return lax.ppermute(v, ("z", "x"), [(i, i ^ k) for i in range(members)])

    fast = n == 4
    spot = (c * n + z) * 2 + x
    pos = [z, x, c, y, m, me]
    if fast:
        partners, sent, held = swap_plan()
        spots = [(i, j, k) for i in range(2) for j in range(n) for k in range(2)]
        table = []
        for i, j, k in spots:
            row = [int(sent[2][i, j, k] == 1 or sent[3][i, j, k] == 2), j * 2 + k]
            for got in held[1:]:
                for line, side in (got[i, j, k], got[1 - i, j, k]):
                    row.append(line * 2 + side)
            table.append(row)
        own_row = jnp.asarray(table, jnp.int32)[spot]
        place_of = jnp.stack(pos).astype(jnp.int32)
        pos = jnp.concatenate([place_of, own_row])
    else:
        pos = place_of = jnp.stack(pos).astype(jnp.int32)
    wide_kv = -(-2 * width // LANES) * LANES
    wide_q = -(-width // LANES) * LANES

    def prep(kinds, wide):
        return whole_call(
            functools.partial(prep_kernel, kinds),
            jax.ShapeDtypeStruct((depth, wide), BF16),
            "sh",
            0,
            2_000_000,
            scratch=[pltpu.VMEM(w_qkv.shape, BF16), pltpu.SemaphoreType.DMA((5,))],
        )(place_of, w_qkv)

    pieces = [prep((1, 2), wide_kv), prep((0,), wide_q)]

    def choose(core, early, late):
        return whole_call(
            functools.partial(choose_kernel, core),
            jax.ShapeDtypeStruct(early.shape, BF16),
            "svv",
            0,
            1_000_000,
        )(pos, early, late)

    def rounds(piece):
        got, both = [piece], []
        for k in range(1, 5):
            give = got[-1]
            if k > 2:
                give = choose(4 - k, got[k - 2], got[k - 1])
            pair = partners[k - 1]
            step = [
                ((i * n + j) * 2 + l, (pair[i, j, l][0] * n + pair[i, j, l][1]) * 2 + pair[i, j, l][2])
                for i, j, l in spots
            ]
            got.append(lax.ppermute(give, ("c", "z", "x"), step))
            both.append((got[k], swap("c", got[k])))
        return both

    own_tokens = latents.reshape(-1, model)
    count = own_tokens.shape[0]
    other_tokens = swap("y", own_tokens)
    far_live = swap("y", frames_live)
    group, plain, old = whole_call(
        functools.partial(table_kernel, heads, rows),
        [
            jax.ShapeDtypeStruct((width, heads * LANES), BF16),
            jax.ShapeDtypeStruct((width, heads * LANES), BF16),
            jax.ShapeDtypeStruct((units, rows, LANES), F32),
        ],
        "svv",
        0,
        2_000_000,
    )(pos, state_in.reshape(units, share, size), ksum_in.reshape(units, size))
    blocks = whole_call(
        block_kernel, jax.ShapeDtypeStruct((members, 2 * count, depth), BF16), "svv", 0, 4_000_000
    )(pos, own_tokens, other_tokens)

    def multiply(slots, acc, *given):
        first = [] if acc is None else [acc]
        wide = given[0].shape[-1]
        return whole_call(
            functools.partial(mul_kernel, slots, acc is None),
            jax.ShapeDtypeStruct((2 * count, wide), F32),
            "sv" + "v" * (len(first) + len(given)),
            1_500_000_000,
            5_000_000,
            alias={2: 0} if first else None,
        )(pos, blocks, *first, *given)

    if fast:
        kvs, qs = rounds(pieces[0]), rounds(pieces[1])
        acc = multiply((7, 8, 9), None, pieces[0], *kvs[0])
        acc = multiply((10, 11), acc, *kvs[1])
        acc = multiply((12, 13), acc, *kvs[2])
        last, last_kv, last_q = ("core",), kvs[3], qs[3]
        asked = multiply((7, 8, 9, 10, 11), None, pieces[1], *qs[0], *qs[1])
        asked = multiply((12, 13), asked, *qs[2])
    else:
        last, last_kv, last_q = ("all",), *(
            (lax.all_gather(piece, ("z", "x"), axis=0, tiled=False),) for piece in pieces
        )
        acc, asked = (jnp.zeros((2 * count, piece.shape[1]), F32) for piece in pieces)

    pairs = 2 * streams * heads
    chunk = jax.ShapeDtypeStruct((pairs, rows, LANES), BF16)
    parts = whole_call(
        functools.partial(kv_kernel, last, streams, frames, heads, size, rows),
        [chunk] * members,
        "sss" + "v" * (4 + len(last_kv)),
        1_500_000_000,
        5_000_000,
        scratch=[pltpu.VMEM(acc.shape, F32)],
    )(pos, frames_live, far_live, blocks, acc, *last_kv, group, plain)
    parts = list(parts)
    q, q_give = whole_call(
        functools.partial(ask_kernel, last, width),
        [
            jax.ShapeDtypeStruct((count, heads * LANES), BF16),
            jax.ShapeDtypeStruct((count, width), BF16),
        ],
        "svvv" + "v" * len(last_q),
        700_000_000,
        3_000_000,
        scratch=[pltpu.VMEM(asked.shape, F32)],
    )(pos, blocks, asked, group, *last_q)

    for k in range(members - 1, 0, -1):
        parts[k] = xor(k, parts[k])
    q_other = swap("y", q_give)

    keep, give = whole_call(
        sum_kernel,
        [
            jax.ShapeDtypeStruct((pairs // 2, rows, LANES), F32),
            jax.ShapeDtypeStruct((pairs // 2, rows, LANES), BF16),
        ],
        "s" + "v" * members,
        0,
        1_000_000,
    )(pos, *parts)
    got = swap("y", give)
    new = whole_call(
        functools.partial(join_kernel, heads),
        jax.ShapeDtypeStruct((units, rows, LANES), BF16),
        "svvv",
        0,
        500_000,
    )(pos, keep, got, old)

    gathered = [new] + [xor(k, new) for k in range(1, members)]
    q_other = whole_call(
        query_kernel,
        jax.ShapeDtypeStruct((count, heads * LANES), BF16),
        "svv",
        140_000_000,
        1_500_000,
    )(pos, q_other, group)

    every, spots, bit = [new], [0], owners // 2
    while bit:
        step = [(i, i ^ bit) for i in range(owners)]
        for i in range(len(every)):
            moved = lax.ppermute(every[i], ("o", "y", "c"), step)
            every.append(moved)
            spots.append(spots[i] ^ bit)
        bit //= 2
    place = whole_call(
        functools.partial(place_kernel, units),
        jax.ShapeDtypeStruct((units,), jnp.int32),
        "ss",
        0,
        1_000,
        smem=True,
    )(pos, new_place)
    moved_state, moved_ksum = whole_call(
        functools.partial(pick_kernel, share, size, rows, spots),
        [
            jax.ShapeDtypeStruct((units, share, size), F32),
            jax.ShapeDtypeStruct((units, size), F32),
        ],
        "s" + "v" * owners,
        1_000_000,
        800_000,
        scratch=[pltpu.VMEM((owners * units, rows, LANES), BF16)],
    )(place, *every)

    attended = whole_call(
        functools.partial(read_kernel, streams, frames, heads, size),
        jax.ShapeDtypeStruct((count, 2 * width), BF16),
        "ssvv" + "v" * members,
        1_500_000_000,
        3_000_000,
    )(pos, frames_live, q, q_other, *gathered)
    return (
        attended.reshape(streams, frames, spatial, 2 * width),
        moved_state,
        moved_ksum,
    )


def solution(mesh):
    owners, members = mesh.shape["req"], mesh.shape["mp"]
    split = Mesh(
        mesh.devices.reshape(owners // 4, 2, 2, members // 2, 2), ("o", "y", "c", "z", "x")
    )
    req, mp = ("o", "y", "c"), ("z", "x")
    return jax.shard_map(
        functools.partial(body, members // 2),
        mesh=split,
        in_specs=(
            P(req, None, mp, None),
            P(mp, None),
            P(req, None, mp, None),
            P(req, None, None),
            P(req),
            P(),
        ),
        out_specs=(P(req, None, mp, None), P(req, mp, None), P(req, None)),
        check_vma=False,
    )
```

```python
import functools

import jax
import jax.numpy as jnp
from jax import lax
from jax.experimental import pallas as pl
from jax.experimental.pallas import tpu as pltpu
from jax.sharding import Mesh
from jax.sharding import PartitionSpec as P


F32 = jnp.float32
BF16 = jnp.bfloat16
LANES = 128
VMEM = pl.BlockSpec(memory_space=pltpu.VMEM)
SMEM = pl.BlockSpec(memory_space=pltpu.SMEM)
SPECS = {"s": SMEM, "v": VMEM, "h": pl.BlockSpec(memory_space=pltpu.HBM)}
SWAP = [(0, 1), (1, 0)]


def swap_plan():
    spots = [(c, z, x) for c in range(2) for z in range(4) for x in range(2)]
    partners, sent, held = [], [], [{(c, z, x): (z, x) for c, z, x in spots}]
    for k in range(1, 5):
        pair, send = {}, {}
        for c, z, x in spots:
            end = z in (0, 3)
            line = (c, z ^ 1, x)
            side = (c, z, 1 - x)
            middle = side if end else (c, 3 - z, x)
            straight = c == (k + 1) % 2
            if k < 3:
                pair[c, z, x] = line if straight else middle
            else:
                pair[c, z, x] = line if straight == (k == 3) else side
            send[c, z, x] = k - 1
            if k == 4:
                pair[c, z, x] = side if c == 0 else line
            if not end and ((k == 3 and c == 1) or (k == 4 and c == 0)):
                send[c, z, x] = k - 2
        partners.append(pair)
        sent.append(send)
        held.append({spot: held[send[pair[spot]]][pair[spot]] for spot in spots})
    return partners, sent, held


def phi(u):
    return jnp.where(u > 0.0, u + 1.0, jnp.exp(jnp.minimum(u, 0.0)))


def whole_call(kernel, out_shape, kinds, flops, moved, scratch=(), alias=None, smem=False, room=20):
    return pl.pallas_call(
        kernel,
        out_shape=out_shape,
        in_specs=[SPECS[kind] for kind in kinds],
        scratch_shapes=scratch,
        input_output_aliases=alias or {},
        out_specs=SMEM if smem else jax.tree.map(lambda _: VMEM, out_shape),
        cost_estimate=pl.CostEstimate(flops=flops, bytes_accessed=moved, transcendentals=0),
        compiler_params=pltpu.CompilerParams(vmem_limit_bytes=room * 1024 * 1024),
    )


def prep_kernel(kinds, pos_ref, w_hbm, out_ref, w_ref, sems):
    depth, total = w_hbm.shape
    width = total // 6
    cuts = sems.shape[0]
    edges = [depth * i // cuts // 8 * 8 for i in range(cuts)] + [depth]
    spans = list(zip(edges, edges[1:]))
    low = min(kinds) * 2 * width // LANES * LANES
    high = min(-(-(max(kinds) + 1) * 2 * width // LANES) * LANES, total)
    copies = []
    for i, (lo, hi) in enumerate(spans):
        if high == total:
            low, source, target = 0, w_hbm.at[lo:hi], w_ref.at[lo:hi]
        else:
            source, target = w_hbm.at[lo:hi, low:high], w_ref.at[lo:hi, : high - low]
        copies.append(pltpu.make_async_copy(source, target, sems.at[i]))
    for copy in copies:
        copy.start()
    used = len(kinds) * width
    if used < out_ref.shape[1]:
        out_ref[:, used:] = jnp.zeros((depth, out_ref.shape[1] - used), BF16)
    for copy, (lo, hi) in zip(copies, spans):
        copy.wait()
        for turn in range(2):

            @pl.when(pos_ref[3] == turn)
            def _():
                for j, kind in enumerate(kinds):
                    start = (2 * kind + turn) * width - low
                    out_ref[lo:hi, j * width : (j + 1) * width] = w_ref[
                        lo:hi, start : start + width
                    ]


def choose_kernel(core, pos_ref, early_ref, late_ref, out_ref):
    early = (pos_ref[6] == 1) & (pos_ref[2] == core)

    @pl.when(early)
    def _():
        out_ref[...] = early_ref[...]

    @pl.when(jnp.logical_not(early))
    def _():
        out_ref[...] = late_ref[...]


def table_kernel(heads, rows, pos_ref, state_ref, ksum_ref, group_ref, plain_ref, old_ref):
    units, share, size = state_ref.shape
    m = pos_ref[4]
    src = lax.broadcasted_iota(jnp.int32, (size, LANES), 0)
    lane = lax.broadcasted_iota(jnp.int32, (size, LANES), 1)
    plain = jnp.where(src == lane, 1.0, 0.0).astype(BF16)
    spot = ((lane // rows) ^ m) * share + lane % rows
    group = jnp.where((src == spot) & (lane % rows < share), 1.0, 0.0).astype(BF16)
    group_ref[...] = jnp.zeros_like(group_ref)
    plain_ref[...] = jnp.zeros_like(plain_ref)
    for h in range(heads):
        group_ref[h * size : (h + 1) * size, h * LANES : (h + 1) * LANES] = group
        plain_ref[h * size : (h + 1) * size, h * LANES : (h + 1) * LANES] = plain
    row = lax.broadcasted_iota(jnp.int32, (rows, size), 0)
    col = lax.broadcasted_iota(jnp.int32, (rows, size), 1)
    chosen = jnp.where((col == m * share + row) & (row < share), 1.0, 0.0)
    ksum = ksum_ref[...]
    turned = lax.dot_general(
        chosen,
        ksum,
        (((1,), (1,)), ((), ())),
        precision=lax.Precision.HIGHEST,
        preferred_element_type=F32,
    )
    old_ref[...] = jnp.zeros_like(old_ref)
    for u in range(units):
        old_ref[u, :, size : size + 1] = turned[:, u : u + 1]
        old_ref[u, :share, :size] = state_ref[u]
        old_ref[u, rows - 1 :, :size] = ksum[u : u + 1]


def block_kernel(pos_ref, own_ref, other_ref, out_ref):
    members, both, _ = out_ref.shape
    count = both // 2
    depth = own_ref.shape[1] // members
    for b in range(members):
        out_ref[b, :count, :depth] = own_ref[:, b * depth : (b + 1) * depth]
        out_ref[b, count:, :depth] = other_ref[:, b * depth : (b + 1) * depth]


def add_products(slots, pos_ref, blocks_ref, refs, tile):
    terms = []
    if slots == ("core",):
        first = pos_ref[2] == 0
        weight = jnp.where(first, refs[0][:, tile], refs[1][:, tile])
        terms = [(jnp.where(first, pos_ref[14], pos_ref[15]), weight)]
    elif slots == ("all",):
        terms = [(b, refs[0][b, :, tile]) for b in range(refs[0].shape[0])]
    else:
        terms = [(pos_ref[slot], ref[:, tile]) for slot, ref in zip(slots, refs)]
    total = None
    for index, weight in terms:
        term = jnp.dot(blocks_ref[index], weight, preferred_element_type=F32)
        total = term if total is None else total + term
    return total


def column_step(wide):
    return next(step for step in (384, 256, LANES) if wide % step == 0)


def mul_kernel(slots, fresh, pos_ref, blocks_ref, *refs):
    acc_ref = refs[-1]
    given = refs[:-1] if fresh else refs[1:-1]
    step = column_step(acc_ref.shape[1])

    @pl.loop(0, acc_ref.shape[1] // step)
    def _(t):
        tile = pl.ds(pl.multiple_of(t * step, step), step)
        term = add_products(slots, pos_ref, blocks_ref, given, tile)
        acc_ref[:, tile] = term if fresh else refs[0][:, tile] + term


def ask_kernel(slots, width, pos_ref, blocks_ref, old_ref, group_ref, *refs):
    given, (mine_ref, give_ref, acc_ref) = refs[:-3], refs[-3:]
    step = column_step(acc_ref.shape[1])

    @pl.loop(0, acc_ref.shape[1] // step)
    def _(t):
        tile = pl.ds(pl.multiple_of(t * step, step), step)
        acc_ref[:, tile] = old_ref[:, tile] + add_products(
            slots, pos_ref, blocks_ref, given, tile
        )

    count = acc_ref.shape[0] // 2
    give_ref[...] = acc_ref[count:, :width].astype(BF16)
    raw = acc_ref[:count, :width].astype(BF16)
    queried = phi(raw.astype(F32)).astype(BF16)
    mine_ref[...] = jnp.dot(queried, group_ref[...], preferred_element_type=F32).astype(BF16)


def kv_kernel(slots, streams, frames, heads, size, rows, pos_ref, near_ref, far_ref, *refs):
    blocks_ref, old_ref, refs = refs[0], refs[1], refs[2:]
    count = 2 if slots == ("core",) else 1
    given, refs = refs[:count], refs[count:]
    group_ref, plain_ref = refs[:2]
    chunks, acc_ref = refs[2:-1], refs[-1]
    step = column_step(acc_ref.shape[1])

    @pl.loop(0, acc_ref.shape[1] // step)
    def _(t):
        tile = pl.ds(pl.multiple_of(t * step, step), step)
        acc_ref[:, tile] = old_ref[:, tile] + add_products(
            slots, pos_ref, blocks_ref, given, tile
        )

    width = heads * size
    count = acc_ref.shape[0] // 2
    tokens = count // streams
    frame = lax.broadcasted_iota(jnp.int32, (tokens, width), 0) // (tokens // frames)
    masks = [frame < ref[s] for ref in (near_ref, far_ref) for s in range(streams)]
    live = jnp.concatenate([jnp.where(mask, 1.0, 0.0) for mask in masks], axis=0)
    keys = acc_ref[:, :width].astype(BF16).astype(F32)
    keyed = (phi(keys) * live).astype(BF16)
    values = acc_ref[:, width : 2 * width].astype(BF16)
    grouped = jnp.dot(keyed, group_ref[...], preferred_element_type=F32).astype(BF16)
    plain = jnp.dot(keyed, plain_ref[...], preferred_element_type=F32)
    spread = jnp.dot(values, plain_ref[...], preferred_element_type=F32)
    lane = lax.broadcasted_iota(jnp.int32, spread.shape, 1) % LANES
    spread = jnp.where(lane == size, 1.0, spread).astype(BF16)
    row = lax.broadcasted_iota(jnp.int32, (LANES, LANES), 0) % rows
    for s in range(2 * streams):
        span = slice(s * tokens, (s + 1) * tokens)
        sums = jnp.sum(plain[span], axis=0, keepdims=True)
        for h in range(heads):
            cols = slice(h * LANES, (h + 1) * LANES)
            outer = lax.dot_general(
                grouped[span, cols],
                spread[span, cols],
                (((0,), (0,)), ((), ())),
                preferred_element_type=F32,
            )
            outer = jnp.where(row == rows - 1, sums[:, cols], outer).astype(BF16)
            for r, chunk in enumerate(chunks):
                chunk[s * heads + h] = outer[r * rows : (r + 1) * rows]


def add_kernel(pos_ref, one_ref, two_ref, out_ref):
    out_ref[...] = (one_ref[...].astype(F32) + two_ref[...].astype(F32)).astype(BF16)


def sum_kernel(*refs):
    parts, keep_ref, give_ref = refs[1:-2], refs[-2], refs[-1]
    half = keep_ref.shape[0]
    for lo, out in ((0, keep_ref), (half, give_ref)):
        total = parts[0][lo : lo + half].astype(F32)
        for part in parts[1:]:
            total = total + part[lo : lo + half].astype(F32)
        out[...] = total.astype(out.dtype)


def join_kernel(heads, pos_ref, keep_ref, got_ref, old_ref, new_ref):
    first = pos_ref[3] == 0
    for s in range(keep_ref.shape[0] // heads):
        keep = keep_ref[s * heads : (s + 1) * heads]
        got = got_ref[s * heads : (s + 1) * heads].astype(F32)
        at = 2 * s * heads
        low = jnp.where(first, keep, got) + old_ref[at : at + heads]
        high = jnp.where(first, got, keep) + old_ref[at + heads : at + 2 * heads]
        new_ref[at : at + heads] = low.astype(BF16)
        new_ref[at + heads : at + 2 * heads] = high.astype(BF16)


def query_kernel(pos_ref, raw_ref, group_ref, out_ref):
    queried = phi(raw_ref[...].astype(F32)).astype(BF16)
    out_ref[...] = jnp.dot(queried, group_ref[...], preferred_element_type=F32).astype(BF16)


def read_kernel(streams, frames, heads, size, pos_ref, near_ref, own_ref, other_ref, *refs):
    pieces, out_ref = refs[:-1], refs[-1]
    tokens = own_ref.shape[0] // streams
    first = pos_ref[3] == 0
    frame = lax.broadcasted_iota(jnp.int32, (tokens, 1), 0) // (tokens // frames)
    own, other = own_ref[...], other_ref[...]
    halves = (jnp.where(first, own, other), jnp.where(first, other, own))
    for s in range(streams):
        span = slice(s * tokens, (s + 1) * tokens)
        live = jnp.where(frame < near_ref[s], 1.0, 0.0)
        for half, grouped in enumerate(halves):
            for h in range(heads):
                pair = s * 2 * heads + half * heads + h
                state = jnp.concatenate([piece[pair] for piece in pieces], axis=0)
                top = jnp.dot(
                    grouped[span, h * LANES : (h + 1) * LANES],
                    state,
                    preferred_element_type=F32,
                )
                result = top[:, :size] / top[:, size : size + 1] * live
                col = (half * heads + h) * size
                out_ref[span, col : col + size] = result.astype(BF16)


def place_kernel(units, pos_ref, new_ref, place_ref):
    me = pos_ref[5]

    @pl.loop(0, new_ref.shape[0])
    def _(g):
        spot = new_ref[g]

        @pl.when(spot // units == me)
        def _():
            place_ref[spot % units] = ((g // units) ^ me) * units + g % units


def pick_kernel(share, size, rows, spots, place_ref, *refs):
    given, (state_ref, ksum_ref, all_ref) = refs[:-3], refs[-3:]
    units = state_ref.shape[0]
    for spot, ref in zip(spots, given):
        all_ref[spot * units : (spot + 1) * units] = ref[...]
    for u in range(units):
        block = all_ref[place_ref[u]].astype(F32)
        state_ref[u] = block[:share, :size]
        ksum_ref[u : u + 1] = block[rows - 1 :, :size]


def body(n, *given):
    return layer(n, *given)


def layer(n, latents, w_qkv, state_in, ksum_in, frames_live, new_place):
    streams, frames, spatial, model = latents.shape
    heads_all, size = ksum_in.shape[1:]
    heads = heads_all // 2
    share = state_in.shape[2]
    members = size // share
    rows = LANES // members
    width = heads * size
    depth = w_qkv.shape[0]
    units = streams * heads_all
    o, y, c = lax.axis_index("o"), lax.axis_index("y"), lax.axis_index("c")
    z, x = lax.axis_index("z"), lax.axis_index("x")
    m = z * 2 + x
    owners = lax.axis_size("o") * 4
    me = (o * 2 + y) * 2 + c

    def swap(axis, v):
        return lax.ppermute(v, axis, SWAP)

    def xor(k, v):
        return lax.ppermute(v, ("z", "x"), [(i, i ^ k) for i in range(members)])

    fast = n == 4
    spot = (c * n + z) * 2 + x
    pos = [z, x, c, y, m, me]
    if fast:
        partners, sent, held = swap_plan()
        spots = [(i, j, k) for i in range(2) for j in range(n) for k in range(2)]
        table = []
        for i, j, k in spots:
            row = [int(sent[2][i, j, k] == 1 or sent[3][i, j, k] == 2), j * 2 + k]
            for got in held[1:]:
                for line, side in (got[i, j, k], got[1 - i, j, k]):
                    row.append(line * 2 + side)
            table.append(row)
        own_row = jnp.asarray(table, jnp.int32)[spot]
        place_of = jnp.stack(pos).astype(jnp.int32)
        pos = jnp.concatenate([place_of, own_row])
    else:
        pos = place_of = jnp.stack(pos).astype(jnp.int32)
    wide_kv = -(-2 * width // LANES) * LANES
    wide_q = -(-width // LANES) * LANES

    def prep(kinds, wide):
        return whole_call(
            functools.partial(prep_kernel, kinds),
            jax.ShapeDtypeStruct((depth, wide), BF16),
            "sh",
            0,
            2_000_000,
            scratch=[pltpu.VMEM(w_qkv.shape, BF16), pltpu.SemaphoreType.DMA((5,))],
            room=60,
        )(place_of, w_qkv)

    pieces = [prep((1, 2), wide_kv), prep((0,), wide_q)]

    def choose(core, early, late):
        return whole_call(
            functools.partial(choose_kernel, core),
            jax.ShapeDtypeStruct(early.shape, BF16),
            "svv",
            0,
            1_000_000,
        )(pos, early, late)

    def rounds(piece):
        got, both = [piece], []
        for k in range(1, 5):
            give = got[-1]
            if k > 2:
                give = choose(4 - k, got[k - 2], got[k - 1])
            pair = partners[k - 1]
            step = [
                ((i * n + j) * 2 + l, (pair[i, j, l][0] * n + pair[i, j, l][1]) * 2 + pair[i, j, l][2])
                for i, j, l in spots
            ]
            got.append(lax.ppermute(give, ("c", "z", "x"), step))
            both.append((got[k], swap("c", got[k])))
        return both

    own_tokens = latents.reshape(-1, model)
    count = own_tokens.shape[0]
    other_tokens = swap("y", own_tokens)
    far_live = swap("y", frames_live)
    group, plain, old = whole_call(
        functools.partial(table_kernel, heads, rows),
        [
            jax.ShapeDtypeStruct((width, heads * LANES), BF16),
            jax.ShapeDtypeStruct((width, heads * LANES), BF16),
            jax.ShapeDtypeStruct((units, rows, LANES), F32),
        ],
        "svv",
        0,
        2_000_000,
    )(pos, state_in.reshape(units, share, size), ksum_in.reshape(units, size))
    blocks = whole_call(
        block_kernel, jax.ShapeDtypeStruct((members, 2 * count, depth), BF16), "svv", 0, 4_000_000
    )(pos, own_tokens, other_tokens)

    def multiply(slots, acc, *given):
        first = [] if acc is None else [acc]
        wide = given[0].shape[-1]
        return whole_call(
            functools.partial(mul_kernel, slots, acc is None),
            jax.ShapeDtypeStruct((2 * count, wide), F32),
            "sv" + "v" * (len(first) + len(given)),
            1_500_000_000,
            5_000_000,
            alias={2: 0} if first else None,
        )(pos, blocks, *first, *given)

    if fast:
        kvs, qs = rounds(pieces[0]), rounds(pieces[1])
        acc = multiply((7, 8, 9), None, pieces[0], *kvs[0])
        acc = multiply((10, 11), acc, *kvs[1])
        acc = multiply((12, 13), acc, *kvs[2])
        last, last_kv, last_q = ("core",), kvs[3], qs[3]
        asked = multiply((7, 8, 9, 10, 11), None, pieces[1], *qs[0], *qs[1])
        asked = multiply((12, 13), asked, *qs[2])
    else:
        last, last_kv, last_q = ("all",), *(
            (lax.all_gather(piece, ("z", "x"), axis=0, tiled=False),) for piece in pieces
        )
        acc, asked = (jnp.zeros((2 * count, piece.shape[1]), F32) for piece in pieces)

    pairs = 2 * streams * heads
    chunk = jax.ShapeDtypeStruct((pairs, rows, LANES), BF16)
    parts = whole_call(
        functools.partial(kv_kernel, last, streams, frames, heads, size, rows),
        [chunk] * members,
        "sss" + "v" * (4 + len(last_kv)),
        1_500_000_000,
        5_000_000,
        scratch=[pltpu.VMEM(acc.shape, F32)],
    )(pos, frames_live, far_live, blocks, acc, *last_kv, group, plain)
    parts = list(parts)
    q, q_give = whole_call(
        functools.partial(ask_kernel, last, width),
        [
            jax.ShapeDtypeStruct((count, heads * LANES), BF16),
            jax.ShapeDtypeStruct((count, width), BF16),
        ],
        "svvv" + "v" * len(last_q),
        700_000_000,
        3_000_000,
        scratch=[pltpu.VMEM(asked.shape, F32)],
    )(pos, blocks, asked, group, *last_q)

    far = members - 1
    parts[far - 1] = whole_call(
        add_kernel, chunk, "svv", 0, 250_000
    )(pos, parts[far - 1], xor(1, parts.pop()))
    for k in range(far - 1, 0, -1):
        parts[k] = xor(k, parts[k])
    q_other = swap("y", q_give)

    keep, give = whole_call(
        sum_kernel,
        [
            jax.ShapeDtypeStruct((pairs // 2, rows, LANES), F32),
            jax.ShapeDtypeStruct((pairs // 2, rows, LANES), BF16),
        ],
        "s" + "v" * far,
        0,
        1_000_000,
    )(pos, *parts)
    got = swap("y", give)
    new = whole_call(
        functools.partial(join_kernel, heads),
        jax.ShapeDtypeStruct((units, rows, LANES), BF16),
        "svvv",
        0,
        500_000,
    )(pos, keep, got, old)

    gathered = [new] + [xor(k, new) for k in range(1, far)]
    gathered.append(xor(1, gathered[far - 1]))
    q_other = whole_call(
        query_kernel,
        jax.ShapeDtypeStruct((count, heads * LANES), BF16),
        "svv",
        140_000_000,
        1_500_000,
    )(pos, q_other, group)

    every, spots, bit = [new], [0], owners // 2
    while bit:
        step = [(i, i ^ bit) for i in range(owners)]
        for i in range(len(every)):
            moved = lax.ppermute(every[i], ("o", "y", "c"), step)
            every.append(moved)
            spots.append(spots[i] ^ bit)
        bit //= 2
    place = whole_call(
        functools.partial(place_kernel, units),
        jax.ShapeDtypeStruct((units,), jnp.int32),
        "ss",
        0,
        1_000,
        smem=True,
    )(pos, new_place)
    moved_state, moved_ksum = whole_call(
        functools.partial(pick_kernel, share, size, rows, spots),
        [
            jax.ShapeDtypeStruct((units, share, size), F32),
            jax.ShapeDtypeStruct((units, size), F32),
        ],
        "s" + "v" * owners,
        1_000_000,
        800_000,
        scratch=[pltpu.VMEM((owners * units, rows, LANES), BF16)],
    )(place, *every)

    attended = whole_call(
        functools.partial(read_kernel, streams, frames, heads, size),
        jax.ShapeDtypeStruct((count, 2 * width), BF16),
        "ssvv" + "v" * members,
        1_500_000_000,
        3_000_000,
    )(pos, frames_live, q, q_other, *gathered)
    return (
        attended.reshape(streams, frames, spatial, 2 * width),
        moved_state,
        moved_ksum,
    )


def solution(mesh):
    owners, members = mesh.shape["req"], mesh.shape["mp"]
    split = Mesh(
        mesh.devices.reshape(owners // 4, 2, 2, members // 2, 2), ("o", "y", "c", "z", "x")
    )
    req, mp = ("o", "y", "c"), ("z", "x")
    return jax.shard_map(
        functools.partial(body, members // 2),
        mesh=split,
        in_specs=(
            P(req, None, mp, None),
            P(mp, None),
            P(req, None, mp, None),
            P(req, None, None),
            P(req),
            P(),
        ),
        out_specs=(P(req, None, mp, None), P(req, mp, None), P(req, None)),
        check_vma=False,
    )
```

```python
import functools

import jax
import jax.numpy as jnp
from jax import lax
from jax.experimental import pallas as pl
from jax.experimental.pallas import tpu as pltpu
from jax.sharding import Mesh
from jax.sharding import PartitionSpec as P


F32 = jnp.float32
BF16 = jnp.bfloat16
LANES = 128
VMEM = pl.BlockSpec(memory_space=pltpu.VMEM)
SMEM = pl.BlockSpec(memory_space=pltpu.SMEM)
SPECS = {"s": SMEM, "v": VMEM, "h": pl.BlockSpec(memory_space=pltpu.HBM)}
SWAP = [(0, 1), (1, 0)]


def swap_plan():
    spots = [(c, z, x) for c in range(2) for z in range(4) for x in range(2)]
    partners, sent, held = [], [], [{(c, z, x): (z, x) for c, z, x in spots}]
    for k in range(1, 5):
        pair, send = {}, {}
        for c, z, x in spots:
            end = z in (0, 3)
            line = (c, z ^ 1, x)
            side = (c, z, 1 - x)
            middle = side if end else (c, 3 - z, x)
            straight = c == (k + 1) % 2
            if k < 3:
                pair[c, z, x] = line if straight else middle
            else:
                pair[c, z, x] = line if straight == (k == 3) else side
            send[c, z, x] = k - 1
            if k == 4:
                pair[c, z, x] = side if c == 0 else line
            if not end and ((k == 3 and c == 1) or (k == 4 and c == 0)):
                send[c, z, x] = k - 2
        partners.append(pair)
        sent.append(send)
        held.append({spot: held[send[pair[spot]]][pair[spot]] for spot in spots})
    return partners, sent, held


def phi(u):
    return jnp.where(u > 0.0, u + 1.0, jnp.exp(jnp.minimum(u, 0.0)))


def whole_call(kernel, out_shape, kinds, flops, moved, scratch=(), alias=None, smem=False, room=20):
    return pl.pallas_call(
        kernel,
        out_shape=out_shape,
        in_specs=[SPECS[kind] for kind in kinds],
        scratch_shapes=scratch,
        input_output_aliases=alias or {},
        out_specs=SMEM if smem else jax.tree.map(lambda _: VMEM, out_shape),
        cost_estimate=pl.CostEstimate(flops=flops, bytes_accessed=moved, transcendentals=0),
        compiler_params=pltpu.CompilerParams(vmem_limit_bytes=room * 1024 * 1024),
    )


def prep_kernel(kinds, pos_ref, w_hbm, out_ref, w_ref, sems):
    depth, total = w_hbm.shape
    width = total // 6
    cuts = sems.shape[0]
    edges = [depth * i // cuts // 8 * 8 for i in range(cuts)] + [depth]
    spans = list(zip(edges, edges[1:]))
    low = min(kinds) * 2 * width // LANES * LANES
    high = min(-(-(max(kinds) + 1) * 2 * width // LANES) * LANES, total)
    copies = []
    for i, (lo, hi) in enumerate(spans):
        if high == total:
            low, source, target = 0, w_hbm.at[lo:hi], w_ref.at[lo:hi]
        else:
            source, target = w_hbm.at[lo:hi, low:high], w_ref.at[lo:hi, : high - low]
        copies.append(pltpu.make_async_copy(source, target, sems.at[i]))
    for copy in copies:
        copy.start()
    used = len(kinds) * width
    if used < out_ref.shape[1]:
        out_ref[:, used:] = jnp.zeros((depth, out_ref.shape[1] - used), BF16)
    for copy, (lo, hi) in zip(copies, spans):
        copy.wait()
        for turn in range(2):

            @pl.when(pos_ref[0] == turn)
            def _():
                for j, kind in enumerate(kinds):
                    start = (2 * kind + turn) * width - low
                    out_ref[lo:hi, j * width : (j + 1) * width] = w_ref[
                        lo:hi, start : start + width
                    ]


def choose_kernel(core, pos_ref, early_ref, late_ref, out_ref):
    early = (pos_ref[6] == 1) & (pos_ref[2] == core)

    @pl.when(early)
    def _():
        out_ref[...] = early_ref[...]

    @pl.when(jnp.logical_not(early))
    def _():
        out_ref[...] = late_ref[...]


def table_kernel(heads, rows, pos_ref, state_ref, ksum_ref, group_ref, plain_ref, old_ref):
    units, share, size = state_ref.shape
    m = pos_ref[4]
    src = lax.broadcasted_iota(jnp.int32, (size, LANES), 0)
    lane = lax.broadcasted_iota(jnp.int32, (size, LANES), 1)
    plain = jnp.where(src == lane, 1.0, 0.0).astype(BF16)
    spot = ((lane // rows) ^ m) * share + lane % rows
    group = jnp.where((src == spot) & (lane % rows < share), 1.0, 0.0).astype(BF16)
    group_ref[...] = jnp.zeros_like(group_ref)
    plain_ref[...] = jnp.zeros_like(plain_ref)
    for h in range(heads):
        group_ref[h * size : (h + 1) * size, h * LANES : (h + 1) * LANES] = group
        plain_ref[h * size : (h + 1) * size, h * LANES : (h + 1) * LANES] = plain
    row = lax.broadcasted_iota(jnp.int32, (rows, size), 0)
    col = lax.broadcasted_iota(jnp.int32, (rows, size), 1)
    chosen = jnp.where((col == m * share + row) & (row < share), 1.0, 0.0)
    ksum = ksum_ref[...]
    turned = lax.dot_general(
        chosen,
        ksum,
        (((1,), (1,)), ((), ())),
        precision=lax.Precision.HIGHEST,
        preferred_element_type=F32,
    )
    old_ref[...] = jnp.zeros_like(old_ref)
    for u in range(units):
        old_ref[u, :, size : size + 1] = turned[:, u : u + 1]
        old_ref[u, :share, :size] = state_ref[u]
        old_ref[u, rows - 1 :, :size] = ksum[u : u + 1]


def block_kernel(pos_ref, own_ref, other_ref, out_ref):
    members, both, _ = out_ref.shape
    count = both // 2
    depth = own_ref.shape[1] // members
    for b in range(members):
        out_ref[b, :count, :depth] = own_ref[:, b * depth : (b + 1) * depth]
        out_ref[b, count:, :depth] = other_ref[:, b * depth : (b + 1) * depth]


def add_products(slots, pos_ref, blocks_ref, refs, tile):
    terms = []
    if slots == ("core",):
        first = pos_ref[2] == 0
        weight = jnp.where(first, refs[0][:, tile], refs[1][:, tile])
        terms = [(jnp.where(first, pos_ref[14], pos_ref[15]), weight)]
    elif slots == ("all",):
        terms = [(b, refs[0][b, :, tile]) for b in range(refs[0].shape[0])]
    else:
        terms = [(pos_ref[slot], ref[:, tile]) for slot, ref in zip(slots, refs)]
    total = None
    for index, weight in terms:
        term = jnp.dot(blocks_ref[index], weight, preferred_element_type=F32)
        total = term if total is None else total + term
    return total


def mul_kernel(slots, fresh, pos_ref, blocks_ref, *refs):
    acc_ref = refs[-1]
    given = refs[:-1] if fresh else refs[1:-1]
    step = acc_ref.shape[1]

    @pl.loop(0, acc_ref.shape[1] // step)
    def _(t):
        tile = pl.ds(pl.multiple_of(t * step, step), step)
        term = add_products(slots, pos_ref, blocks_ref, given, tile)
        acc_ref[:, tile] = term if fresh else refs[0][:, tile] + term


def ask_kernel(slots, width, pos_ref, blocks_ref, old_ref, group_ref, *refs):
    given, (mine_ref, give_ref, acc_ref) = refs[:-3], refs[-3:]
    step = acc_ref.shape[1]

    @pl.loop(0, acc_ref.shape[1] // step)
    def _(t):
        tile = pl.ds(pl.multiple_of(t * step, step), step)
        acc_ref[:, tile] = old_ref[:, tile] + add_products(
            slots, pos_ref, blocks_ref, given, tile
        )

    count = acc_ref.shape[0] // 2
    give_ref[...] = acc_ref[count:, :width].astype(BF16)
    raw = acc_ref[:count, :width].astype(BF16)
    queried = phi(raw.astype(F32)).astype(BF16)
    mine_ref[...] = jnp.dot(queried, group_ref[...], preferred_element_type=F32).astype(BF16)


def kv_kernel(slots, streams, frames, heads, size, rows, pos_ref, near_ref, far_ref, *refs):
    blocks_ref, old_ref, refs = refs[0], refs[1], refs[2:]
    count = 2 if slots == ("core",) else 1
    given, refs = refs[:count], refs[count:]
    group_ref, plain_ref = refs[:2]
    chunks, acc_ref = refs[2:-1], refs[-1]
    step = acc_ref.shape[1]

    @pl.loop(0, acc_ref.shape[1] // step)
    def _(t):
        tile = pl.ds(pl.multiple_of(t * step, step), step)
        acc_ref[:, tile] = old_ref[:, tile] + add_products(
            slots, pos_ref, blocks_ref, given, tile
        )

    width = heads * size
    count = acc_ref.shape[0] // 2
    tokens = count // streams
    frame = lax.broadcasted_iota(jnp.int32, (tokens, width), 0) // (tokens // frames)
    masks = [frame < ref[s] for ref in (near_ref, far_ref) for s in range(streams)]
    live = jnp.concatenate([jnp.where(mask, 1.0, 0.0) for mask in masks], axis=0)
    keys = acc_ref[:, :width].astype(BF16).astype(F32)
    keyed = (phi(keys) * live).astype(BF16)
    values = acc_ref[:, width : 2 * width].astype(BF16)
    grouped = jnp.dot(keyed, group_ref[...], preferred_element_type=F32).astype(BF16)
    plain = jnp.dot(keyed, plain_ref[...], preferred_element_type=F32)
    spread = jnp.dot(values, plain_ref[...], preferred_element_type=F32)
    lane = lax.broadcasted_iota(jnp.int32, spread.shape, 1) % LANES
    spread = jnp.where(lane == size, 1.0, spread).astype(BF16)
    row = lax.broadcasted_iota(jnp.int32, (LANES, LANES), 0) % rows
    for s in range(2 * streams):
        span = slice(s * tokens, (s + 1) * tokens)
        sums = jnp.sum(plain[span], axis=0, keepdims=True)
        for h in range(heads):
            cols = slice(h * LANES, (h + 1) * LANES)
            outer = lax.dot_general(
                grouped[span, cols],
                spread[span, cols],
                (((0,), (0,)), ((), ())),
                preferred_element_type=F32,
            )
            outer = jnp.where(row == rows - 1, sums[:, cols], outer).astype(BF16)
            for r, chunk in enumerate(chunks):
                chunk[s * heads + h] = outer[r * rows : (r + 1) * rows]


def add_kernel(pos_ref, one_ref, two_ref, out_ref):
    out_ref[...] = (one_ref[...].astype(F32) + two_ref[...].astype(F32)).astype(BF16)


def sum_kernel(*refs):
    parts, keep_ref, give_ref = refs[1:-2], refs[-2], refs[-1]
    half = keep_ref.shape[0]
    for lo, out in ((0, keep_ref), (half, give_ref)):
        total = parts[0][lo : lo + half].astype(F32)
        for part in parts[1:]:
            total = total + part[lo : lo + half].astype(F32)
        out[...] = total.astype(out.dtype)


def join_kernel(heads, pos_ref, keep_ref, got_ref, old_ref, new_ref):
    first = pos_ref[3] == 0
    for s in range(keep_ref.shape[0] // heads):
        keep = keep_ref[s * heads : (s + 1) * heads]
        got = got_ref[s * heads : (s + 1) * heads].astype(F32)
        at = 2 * s * heads
        low = jnp.where(first, keep, got) + old_ref[at : at + heads]
        high = jnp.where(first, got, keep) + old_ref[at + heads : at + 2 * heads]
        new_ref[at : at + heads] = low.astype(BF16)
        new_ref[at + heads : at + 2 * heads] = high.astype(BF16)


def query_kernel(pos_ref, raw_ref, group_ref, out_ref):
    queried = phi(raw_ref[...].astype(F32)).astype(BF16)
    out_ref[...] = jnp.dot(queried, group_ref[...], preferred_element_type=F32).astype(BF16)


def read_kernel(streams, frames, heads, size, pos_ref, near_ref, own_ref, other_ref, *refs):
    pieces, out_ref = refs[:-1], refs[-1]
    tokens = own_ref.shape[0] // streams
    first = pos_ref[3] == 0
    frame = lax.broadcasted_iota(jnp.int32, (tokens, 1), 0) // (tokens // frames)
    own, other = own_ref[...], other_ref[...]
    halves = (jnp.where(first, own, other), jnp.where(first, other, own))
    for s in range(streams):
        span = slice(s * tokens, (s + 1) * tokens)
        live = jnp.where(frame < near_ref[s], 1.0, 0.0)
        for half, grouped in enumerate(halves):
            for h in range(heads):
                pair = s * 2 * heads + half * heads + h
                state = jnp.concatenate([piece[pair] for piece in pieces], axis=0)
                top = jnp.dot(
                    grouped[span, h * LANES : (h + 1) * LANES],
                    state,
                    preferred_element_type=F32,
                )
                result = top[:, :size] / top[:, size : size + 1] * live
                col = (half * heads + h) * size
                out_ref[span, col : col + size] = result.astype(BF16)


def place_kernel(units, pos_ref, new_ref, place_ref):
    me = pos_ref[5]

    @pl.loop(0, new_ref.shape[0])
    def _(g):
        spot = new_ref[g]

        @pl.when(spot // units == me)
        def _():
            place_ref[spot % units] = ((g // units) ^ me) * units + g % units


def pick_kernel(share, size, rows, spots, place_ref, *refs):
    given, (state_ref, ksum_ref, all_ref) = refs[:-3], refs[-3:]
    units = state_ref.shape[0]
    for spot, ref in zip(spots, given):
        all_ref[spot * units : (spot + 1) * units] = ref[...]
    for u in range(units):
        block = all_ref[place_ref[u]].astype(F32)
        state_ref[u] = block[:share, :size]
        ksum_ref[u : u + 1] = block[rows - 1 :, :size]


def body(n, *given):
    return layer(n, *given)


def layer(n, latents, w_qkv, state_in, ksum_in, frames_live, new_place):
    streams, frames, spatial, model = latents.shape
    heads_all, size = ksum_in.shape[1:]
    heads = heads_all // 2
    share = state_in.shape[2]
    members = size // share
    rows = LANES // members
    width = heads * size
    depth = w_qkv.shape[0]
    units = streams * heads_all
    o, y, c = lax.axis_index("o"), lax.axis_index("y"), lax.axis_index("c")
    z, x = lax.axis_index("z"), lax.axis_index("x")
    m = z * 2 + x
    owners = lax.axis_size("o") * 4
    me = (o * 2 + y) * 2 + c

    def swap(axis, v):
        return lax.ppermute(v, axis, SWAP)

    def xor(k, v):
        return lax.ppermute(v, ("z", "x"), [(i, i ^ k) for i in range(members)])

    fast = n == 4
    spot = (c * n + z) * 2 + x
    pos = [z, x, c, y, m, me]
    if fast:
        partners, sent, held = swap_plan()
        spots = [(i, j, k) for i in range(2) for j in range(n) for k in range(2)]
        table = []
        for i, j, k in spots:
            row = [int(sent[2][i, j, k] == 1 or sent[3][i, j, k] == 2), j * 2 + k]
            for got in held[1:]:
                for line, side in (got[i, j, k], got[1 - i, j, k]):
                    row.append(line * 2 + side)
            table.append(row)
        own_row = jnp.asarray(table, jnp.int32)[spot]
        place_of = jnp.stack(pos).astype(jnp.int32)
        pos = jnp.concatenate([place_of, own_row])
    else:
        pos = place_of = jnp.stack(pos).astype(jnp.int32)
    wide_kv = -(-2 * width // LANES) * LANES
    wide_q = -(-width // LANES) * LANES

    def prep(kinds, wide):
        return whole_call(
            functools.partial(prep_kernel, kinds),
            jax.ShapeDtypeStruct((depth, wide), BF16),
            "sh",
            0,
            2_000_000,
            scratch=[pltpu.VMEM(w_qkv.shape, BF16), pltpu.SemaphoreType.DMA((5,))],
        )(y.reshape(1), pltpu.with_memory_space_constraint(w_qkv, pltpu.HBM))

    pieces = [prep((1, 2), wide_kv), prep((0,), wide_q)]

    def choose(core, early, late):
        return whole_call(
            functools.partial(choose_kernel, core),
            jax.ShapeDtypeStruct(early.shape, BF16),
            "svv",
            0,
            1_000_000,
        )(pos, early, late)

    def rounds(piece):
        got, both = [piece], []
        for k in range(1, 5):
            give = got[-1]
            if k > 2:
                give = choose(4 - k, got[k - 2], got[k - 1])
            pair = partners[k - 1]
            step = [
                ((i * n + j) * 2 + l, (pair[i, j, l][0] * n + pair[i, j, l][1]) * 2 + pair[i, j, l][2])
                for i, j, l in spots
            ]
            got.append(lax.ppermute(give, ("c", "z", "x"), step))
            both.append((got[k], swap("c", got[k])))
        return both

    own_tokens = latents.reshape(-1, model)
    count = own_tokens.shape[0]
    other_tokens = swap("y", own_tokens)
    far_live = swap("y", frames_live)
    group, plain, old = whole_call(
        functools.partial(table_kernel, heads, rows),
        [
            jax.ShapeDtypeStruct((width, heads * LANES), BF16),
            jax.ShapeDtypeStruct((width, heads * LANES), BF16),
            jax.ShapeDtypeStruct((units, rows, LANES), F32),
        ],
        "svv",
        0,
        2_000_000,
    )(pos, state_in.reshape(units, share, size), ksum_in.reshape(units, size))
    blocks = whole_call(
        block_kernel, jax.ShapeDtypeStruct((members, 2 * count, depth), BF16), "svv", 0, 4_000_000
    )(pos, own_tokens, other_tokens)

    def multiply(slots, acc, *given):
        first = [] if acc is None else [acc]
        wide = given[0].shape[-1]
        return whole_call(
            functools.partial(mul_kernel, slots, acc is None),
            jax.ShapeDtypeStruct((2 * count, wide), F32),
            "sv" + "v" * (len(first) + len(given)),
            1_500_000_000,
            5_000_000,
            alias={2: 0} if first else None,
        )(pos, blocks, *first, *given)

    if fast:
        kvs, qs = rounds(pieces[0]), rounds(pieces[1])
        acc = multiply((7, 8, 9), None, pieces[0], *kvs[0])
        acc = multiply((10, 11), acc, *kvs[1])
        acc = multiply((12, 13), acc, *kvs[2])
        last, last_kv, last_q = ("core",), kvs[3], qs[3]
        asked = multiply((7, 8, 9, 10, 11), None, pieces[1], *qs[0], *qs[1])
        asked = multiply((12, 13), asked, *qs[2])
    else:
        last, last_kv, last_q = ("all",), *(
            (lax.all_gather(piece, ("z", "x"), axis=0, tiled=False),) for piece in pieces
        )
        acc, asked = (jnp.zeros((2 * count, piece.shape[1]), F32) for piece in pieces)

    pairs = 2 * streams * heads
    chunk = jax.ShapeDtypeStruct((pairs, rows, LANES), BF16)
    parts = whole_call(
        functools.partial(kv_kernel, last, streams, frames, heads, size, rows),
        [chunk] * members,
        "sss" + "v" * (4 + len(last_kv)),
        1_500_000_000,
        5_000_000,
        scratch=[pltpu.VMEM(acc.shape, F32)],
    )(pos, frames_live, far_live, blocks, acc, *last_kv, group, plain)
    parts = list(parts)
    q, q_give = whole_call(
        functools.partial(ask_kernel, last, width),
        [
            jax.ShapeDtypeStruct((count, heads * LANES), BF16),
            jax.ShapeDtypeStruct((count, width), BF16),
        ],
        "svvv" + "v" * len(last_q),
        700_000_000,
        3_000_000,
        scratch=[pltpu.VMEM(asked.shape, F32)],
    )(pos, blocks, asked, group, *last_q)

    far = members - 1
    parts[far - 1] = whole_call(
        add_kernel, chunk, "svv", 0, 250_000
    )(pos, parts[far - 1], xor(1, parts.pop()))
    for k in range(far - 1, 0, -1):
        parts[k] = xor(k, parts[k])
    q_other = swap("y", q_give)

    keep, give = whole_call(
        sum_kernel,
        [
            jax.ShapeDtypeStruct((pairs // 2, rows, LANES), F32),
            jax.ShapeDtypeStruct((pairs // 2, rows, LANES), BF16),
        ],
        "s" + "v" * far,
        0,
        1_000_000,
    )(pos, *parts)
    got = swap("y", give)
    new = whole_call(
        functools.partial(join_kernel, heads),
        jax.ShapeDtypeStruct((units, rows, LANES), BF16),
        "svvv",
        0,
        500_000,
    )(pos, keep, got, old)

    gathered = [new] + [xor(k, new) for k in range(1, far)]
    gathered.append(xor(1, gathered[far - 1]))
    q_other = whole_call(
        query_kernel,
        jax.ShapeDtypeStruct((count, heads * LANES), BF16),
        "svv",
        140_000_000,
        1_500_000,
    )(pos, q_other, group)

    every, spots, bit = [new], [0], owners // 2
    while bit:
        step = [(i, i ^ bit) for i in range(owners)]
        for i in range(len(every)):
            moved = lax.ppermute(every[i], ("o", "y", "c"), step)
            every.append(moved)
            spots.append(spots[i] ^ bit)
        bit //= 2
    place = whole_call(
        functools.partial(place_kernel, units),
        jax.ShapeDtypeStruct((units,), jnp.int32),
        "ss",
        0,
        1_000,
        smem=True,
    )(pos, new_place)
    moved_state, moved_ksum = whole_call(
        functools.partial(pick_kernel, share, size, rows, spots),
        [
            jax.ShapeDtypeStruct((units, share, size), F32),
            jax.ShapeDtypeStruct((units, size), F32),
        ],
        "s" + "v" * owners,
        1_000_000,
        800_000,
        scratch=[pltpu.VMEM((owners * units, rows, LANES), BF16)],
    )(place, *every)

    attended = whole_call(
        functools.partial(read_kernel, streams, frames, heads, size),
        jax.ShapeDtypeStruct((count, 2 * width), BF16),
        "ssvv" + "v" * members,
        1_500_000_000,
        3_000_000,
    )(pos, frames_live, q, q_other, *gathered)
    return (
        attended.reshape(streams, frames, spatial, 2 * width),
        moved_state,
        moved_ksum,
    )


def solution(mesh):
    owners, members = mesh.shape["req"], mesh.shape["mp"]
    split = Mesh(
        mesh.devices.reshape(owners // 4, 2, 2, members // 2, 2), ("o", "y", "c", "z", "x")
    )
    req, mp = ("o", "y", "c"), ("z", "x")
    return jax.shard_map(
        functools.partial(body, members // 2),
        mesh=split,
        in_specs=(
            P(req, None, mp, None),
            P(mp, None),
            P(req, None, mp, None),
            P(req, None, None),
            P(req),
            P(),
        ),
        out_specs=(P(req, None, mp, None), P(req, mp, None), P(req, None)),
        check_vma=False,
    )
```

```python
import functools

import jax
import jax.numpy as jnp
from jax import lax
from jax.experimental import pallas as pl
from jax.experimental.pallas import tpu as pltpu
from jax.sharding import Mesh
from jax.sharding import PartitionSpec as P


F32 = jnp.float32
BF16 = jnp.bfloat16
LANES = 128
VMEM = pl.BlockSpec(memory_space=pltpu.VMEM)
SMEM = pl.BlockSpec(memory_space=pltpu.SMEM)
SPECS = {"s": SMEM, "v": VMEM, "h": pl.BlockSpec(memory_space=pltpu.HBM)}
SWAP = [(0, 1), (1, 0)]


def swap_plan():
    spots = [(c, z, x) for c in range(2) for z in range(4) for x in range(2)]
    partners, sent, held = [], [], [{(c, z, x): (z, x) for c, z, x in spots}]
    for k in range(1, 5):
        pair, send = {}, {}
        for c, z, x in spots:
            end = z in (0, 3)
            line = (c, z ^ 1, x)
            side = (c, z, 1 - x)
            middle = side if end else (c, 3 - z, x)
            straight = c == (k + 1) % 2
            if k < 3:
                pair[c, z, x] = line if straight else middle
            else:
                pair[c, z, x] = line if straight == (k == 3) else side
            send[c, z, x] = k - 1
            if k == 4:
                pair[c, z, x] = side if c == 0 else line
            if not end and ((k == 3 and c == 1) or (k == 4 and c == 0)):
                send[c, z, x] = k - 2
        partners.append(pair)
        sent.append(send)
        held.append({spot: held[send[pair[spot]]][pair[spot]] for spot in spots})
    return partners, sent, held


def phi(u):
    return jnp.where(u > 0.0, u + 1.0, jnp.exp(jnp.minimum(u, 0.0)))


def whole_call(kernel, out_shape, kinds, flops, moved, scratch=(), alias=None, smem=False, room=20):
    return pl.pallas_call(
        kernel,
        out_shape=out_shape,
        in_specs=[SPECS[kind] for kind in kinds],
        scratch_shapes=scratch,
        input_output_aliases=alias or {},
        out_specs=SMEM if smem else jax.tree.map(lambda _: VMEM, out_shape),
        cost_estimate=pl.CostEstimate(flops=flops, bytes_accessed=moved, transcendentals=0),
        compiler_params=pltpu.CompilerParams(vmem_limit_bytes=room * 1024 * 1024),
    )


def prep_kernel(kinds, first, last, pos_ref, w_hbm, out_ref, w_ref, sems):
    total = w_hbm.shape[1]
    width = total // 6
    high = min(-(-(max(kinds) + 1) * 2 * width // LANES) * LANES, total)
    mid = (last - first) // 32 * 16
    spans = [(0, mid), (mid, last - first)]
    copies = []
    for i, (lo, hi) in enumerate(spans):
        if high == total:
            source, target = w_hbm.at[first + lo : first + hi], w_ref.at[lo:hi]
        else:
            source = w_hbm.at[first + lo : first + hi, :high]
            target = w_ref.at[lo:hi, :high]
        copies.append(pltpu.make_async_copy(source, target, sems.at[i]))
    for copy in copies:
        copy.start()
    used = len(kinds) * width
    if used < out_ref.shape[1]:
        out_ref[:, used:] = jnp.zeros((last - first, out_ref.shape[1] - used), BF16)
    for copy, (lo, hi) in zip(copies, spans):
        copy.wait()
        for turn in range(2):

            @pl.when(pos_ref[0] == turn)
            def _():
                for j, kind in enumerate(kinds):
                    start = (2 * kind + turn) * width
                    out_ref[lo:hi, j * width : (j + 1) * width] = w_ref[
                        lo:hi, start : start + width
                    ]


def choose_kernel(core, pos_ref, early_ref, late_ref, out_ref):
    early = (pos_ref[6] == 1) & (pos_ref[2] == core)

    @pl.when(early)
    def _():
        out_ref[...] = early_ref[...]

    @pl.when(jnp.logical_not(early))
    def _():
        out_ref[...] = late_ref[...]


def table_kernel(heads, rows, pos_ref, state_ref, ksum_ref, group_ref, plain_ref, old_ref):
    units, share, size = state_ref.shape
    m = pos_ref[4]
    src = lax.broadcasted_iota(jnp.int32, (size, LANES), 0)
    lane = lax.broadcasted_iota(jnp.int32, (size, LANES), 1)
    plain = jnp.where(src == lane, 1.0, 0.0).astype(BF16)
    spot = ((lane // rows) ^ m) * share + lane % rows
    group = jnp.where((src == spot) & (lane % rows < share), 1.0, 0.0).astype(BF16)
    group_ref[...] = jnp.zeros_like(group_ref)
    plain_ref[...] = jnp.zeros_like(plain_ref)
    for h in range(heads):
        group_ref[h * size : (h + 1) * size, h * LANES : (h + 1) * LANES] = group
        plain_ref[h * size : (h + 1) * size, h * LANES : (h + 1) * LANES] = plain
    row = lax.broadcasted_iota(jnp.int32, (rows, size), 0)
    col = lax.broadcasted_iota(jnp.int32, (rows, size), 1)
    chosen = jnp.where((col == m * share + row) & (row < share), 1.0, 0.0)
    ksum = ksum_ref[...]
    turned = lax.dot_general(
        chosen,
        ksum,
        (((1,), (1,)), ((), ())),
        precision=lax.Precision.HIGHEST,
        preferred_element_type=F32,
    )
    old_ref[...] = jnp.zeros_like(old_ref)
    for u in range(units):
        old_ref[u, :, size : size + 1] = turned[:, u : u + 1]
        old_ref[u, :share, :size] = state_ref[u]
        old_ref[u, rows - 1 :, :size] = ksum[u : u + 1]


def block_kernel(pos_ref, own_ref, other_ref, lead_ref, tail_ref):
    members, both, half = lead_ref.shape
    count = both // 2
    depth = own_ref.shape[1] // members
    for b in range(members):
        for span, ref in ((slice(0, count), own_ref), (slice(count, both), other_ref)):
            lead_ref[b, span] = ref[:, b * depth : b * depth + half]
            tail_ref[b, span] = ref[:, b * depth + half : (b + 1) * depth]


def add_products(slots, split, pos_ref, lead_ref, tail_ref, refs, tile):
    half = lead_ref.shape[2]

    def rows(i, *at):
        if split:
            return refs[2 * i][*at, :, tile], refs[2 * i + 1][*at, :, tile]
        return refs[i][*at, :half, tile], refs[i][*at, half:, tile]

    if slots == ("core",):
        first = pos_ref[2] == 0
        weights = [jnp.where(first, a, b) for a, b in zip(rows(0), rows(1))]
        terms = [(jnp.where(first, pos_ref[14], pos_ref[15]), weights)]
    elif slots == ("all",):
        terms = [(b, rows(0, b)) for b in range(refs[0].shape[0])]
    else:
        terms = [(pos_ref[slot], rows(i)) for i, slot in enumerate(slots)]
    total = None
    for index, (lead, tail) in terms:
        for lhs, weight in ((lead_ref, lead), (tail_ref, tail)):
            term = jnp.dot(lhs[index], weight, preferred_element_type=F32)
            total = term if total is None else total + term
    return total


def mul_kernel(slots, split, fresh, pos_ref, lead_ref, tail_ref, *refs):
    acc_ref = refs[-1]
    given = refs[:-1] if fresh else refs[1:-1]
    step = acc_ref.shape[1]

    @pl.loop(0, acc_ref.shape[1] // step)
    def _(t):
        tile = pl.ds(pl.multiple_of(t * step, step), step)
        term = add_products(slots, split, pos_ref, lead_ref, tail_ref, given, tile)
        acc_ref[:, tile] = term if fresh else refs[0][:, tile] + term


def ask_kernel(slots, width, pos_ref, lead_ref, tail_ref, old_ref, group_ref, *refs):
    given, (mine_ref, give_ref, acc_ref) = refs[:-3], refs[-3:]
    step = acc_ref.shape[1]

    @pl.loop(0, acc_ref.shape[1] // step)
    def _(t):
        tile = pl.ds(pl.multiple_of(t * step, step), step)
        acc_ref[:, tile] = old_ref[:, tile] + add_products(
            slots, False, pos_ref, lead_ref, tail_ref, given, tile
        )

    count = acc_ref.shape[0] // 2
    give_ref[...] = acc_ref[count:, :width].astype(BF16)
    raw = acc_ref[:count, :width].astype(BF16)
    queried = phi(raw.astype(F32)).astype(BF16)
    mine_ref[...] = jnp.dot(queried, group_ref[...], preferred_element_type=F32).astype(BF16)


def kv_kernel(slots, streams, frames, heads, size, rows, pos_ref, near_ref, far_ref, *refs):
    lead_ref, tail_ref, old_ref, refs = refs[0], refs[1], refs[2], refs[3:]
    count = 4 if slots == ("core",) else 2
    given, refs = refs[:count], refs[count:]
    group_ref, plain_ref = refs[:2]
    chunks, acc_ref = refs[2:-1], refs[-1]
    step = acc_ref.shape[1]

    @pl.loop(0, acc_ref.shape[1] // step)
    def _(t):
        tile = pl.ds(pl.multiple_of(t * step, step), step)
        acc_ref[:, tile] = old_ref[:, tile] + add_products(
            slots, True, pos_ref, lead_ref, tail_ref, given, tile
        )

    width = heads * size
    count = acc_ref.shape[0] // 2
    tokens = count // streams
    frame = lax.broadcasted_iota(jnp.int32, (tokens, width), 0) // (tokens // frames)
    masks = [frame < ref[s] for ref in (near_ref, far_ref) for s in range(streams)]
    live = jnp.concatenate([jnp.where(mask, 1.0, 0.0) for mask in masks], axis=0)
    keys = acc_ref[:, :width].astype(BF16).astype(F32)
    keyed = (phi(keys) * live).astype(BF16)
    values = acc_ref[:, width : 2 * width].astype(BF16)
    grouped = jnp.dot(keyed, group_ref[...], preferred_element_type=F32).astype(BF16)
    plain = jnp.dot(keyed, plain_ref[...], preferred_element_type=F32)
    spread = jnp.dot(values, plain_ref[...], preferred_element_type=F32)
    lane = lax.broadcasted_iota(jnp.int32, spread.shape, 1) % LANES
    spread = jnp.where(lane == size, 1.0, spread).astype(BF16)
    row = lax.broadcasted_iota(jnp.int32, (LANES, LANES), 0) % rows
    for s in range(2 * streams):
        span = slice(s * tokens, (s + 1) * tokens)
        sums = jnp.sum(plain[span], axis=0, keepdims=True)
        for h in range(heads):
            cols = slice(h * LANES, (h + 1) * LANES)
            outer = lax.dot_general(
                grouped[span, cols],
                spread[span, cols],
                (((0,), (0,)), ((), ())),
                preferred_element_type=F32,
            )
            outer = jnp.where(row == rows - 1, sums[:, cols], outer).astype(BF16)
            for r, chunk in enumerate(chunks):
                chunk[s * heads + h] = outer[r * rows : (r + 1) * rows]


def add_kernel(pos_ref, one_ref, two_ref, out_ref):
    out_ref[...] = (one_ref[...].astype(F32) + two_ref[...].astype(F32)).astype(BF16)


def sum_kernel(*refs):
    parts, keep_ref, give_ref = refs[1:-2], refs[-2], refs[-1]
    half = keep_ref.shape[0]
    for lo, out in ((0, keep_ref), (half, give_ref)):
        total = parts[0][lo : lo + half].astype(F32)
        for part in parts[1:]:
            total = total + part[lo : lo + half].astype(F32)
        out[...] = total.astype(out.dtype)


def join_kernel(heads, pos_ref, keep_ref, got_ref, old_ref, new_ref):
    first = pos_ref[3] == 0
    for s in range(keep_ref.shape[0] // heads):
        keep = keep_ref[s * heads : (s + 1) * heads]
        got = got_ref[s * heads : (s + 1) * heads].astype(F32)
        at = 2 * s * heads
        low = jnp.where(first, keep, got) + old_ref[at : at + heads]
        high = jnp.where(first, got, keep) + old_ref[at + heads : at + 2 * heads]
        new_ref[at : at + heads] = low.astype(BF16)
        new_ref[at + heads : at + 2 * heads] = high.astype(BF16)


def query_kernel(pos_ref, raw_ref, group_ref, out_ref):
    queried = phi(raw_ref[...].astype(F32)).astype(BF16)
    out_ref[...] = jnp.dot(queried, group_ref[...], preferred_element_type=F32).astype(BF16)


def read_kernel(streams, frames, heads, size, pos_ref, near_ref, own_ref, other_ref, *refs):
    pieces, out_ref = refs[:-1], refs[-1]
    tokens = own_ref.shape[0] // streams
    first = pos_ref[3] == 0
    frame = lax.broadcasted_iota(jnp.int32, (tokens, 1), 0) // (tokens // frames)
    own, other = own_ref[...], other_ref[...]
    halves = (jnp.where(first, own, other), jnp.where(first, other, own))
    for s in range(streams):
        span = slice(s * tokens, (s + 1) * tokens)
        live = jnp.where(frame < near_ref[s], 1.0, 0.0)
        for half, grouped in enumerate(halves):
            for h in range(heads):
                pair = s * 2 * heads + half * heads + h
                state = jnp.concatenate([piece[pair] for piece in pieces], axis=0)
                top = jnp.dot(
                    grouped[span, h * LANES : (h + 1) * LANES],
                    state,
                    preferred_element_type=F32,
                )
                result = top[:, :size] / top[:, size : size + 1] * live
                col = (half * heads + h) * size
                out_ref[span, col : col + size] = result.astype(BF16)


def place_kernel(units, pos_ref, new_ref, place_ref):
    me = pos_ref[5]

    @pl.loop(0, new_ref.shape[0] // units)
    def _(owner):
        first = (owner ^ me) * units
        for local in range(units):
            spot = new_ref[owner * units + local] - me * units

            @pl.when((spot >= 0) & (spot < units))
            def _():
                place_ref[spot] = first + local


def pick_kernel(share, size, rows, spots, place_ref, *refs):
    given, (state_ref, ksum_ref, all_ref) = refs[:-3], refs[-3:]
    units = state_ref.shape[0]
    for spot, ref in zip(spots, given):
        all_ref[spot * units : (spot + 1) * units] = ref[...]
    for u in range(units):
        block = all_ref[place_ref[u]].astype(F32)
        state_ref[u] = block[:share, :size]
        ksum_ref[u : u + 1] = block[rows - 1 :, :size]


def body(n, *given):
    return layer(n, *given)


def layer(n, latents, w_qkv, state_in, ksum_in, frames_live, new_place):
    streams, frames, spatial, model = latents.shape
    heads_all, size = ksum_in.shape[1:]
    heads = heads_all // 2
    share = state_in.shape[2]
    members = size // share
    rows = LANES // members
    width = heads * size
    depth = w_qkv.shape[0]
    units = streams * heads_all
    o, y, c = lax.axis_index("o"), lax.axis_index("y"), lax.axis_index("c")
    z, x = lax.axis_index("z"), lax.axis_index("x")
    m = z * 2 + x
    owners = lax.axis_size("o") * 4
    me = (o * 2 + y) * 2 + c

    def swap(axis, v):
        return lax.ppermute(v, axis, SWAP)

    def xor(k, v):
        return lax.ppermute(v, ("z", "x"), [(i, i ^ k) for i in range(members)])

    fast = n == 4
    spot = (c * n + z) * 2 + x
    pos = [z, x, c, y, m, me]
    if fast:
        partners, sent, held = swap_plan()
        spots = [(i, j, k) for i in range(2) for j in range(n) for k in range(2)]
        table = []
        for i, j, k in spots:
            row = [int(sent[2][i, j, k] == 1 or sent[3][i, j, k] == 2), j * 2 + k]
            for got in held[1:]:
                for line, side in (got[i, j, k], got[1 - i, j, k]):
                    row.append(line * 2 + side)
            table.append(row)
        own_row = jnp.asarray(table, jnp.int32)[spot]
        place_of = jnp.stack(pos).astype(jnp.int32)
        pos = jnp.concatenate([place_of, own_row])
    else:
        pos = place_of = jnp.stack(pos).astype(jnp.int32)
    wide_kv = -(-2 * width // LANES) * LANES
    wide_q = -(-width // LANES) * LANES

    half = -(-depth // 32) * 16

    def prep(kinds, wide, first, last):
        return whole_call(
            functools.partial(prep_kernel, kinds, first, last),
            jax.ShapeDtypeStruct((last - first, wide), BF16),
            "sh",
            0,
            2_000_000,
            scratch=[
                pltpu.VMEM((last - first, w_qkv.shape[1]), BF16),
                pltpu.SemaphoreType.DMA((2,)),
            ],
        )(y.reshape(1), pltpu.with_memory_space_constraint(w_qkv, pltpu.HBM))

    leads = prep((1, 2), wide_kv, 0, half)
    tails = prep((1, 2), wide_kv, half, depth)
    wholes = prep((0,), wide_q, 0, depth)

    def choose(core, early, late):
        return whole_call(
            functools.partial(choose_kernel, core),
            jax.ShapeDtypeStruct(early.shape, BF16),
            "svv",
            0,
            1_000_000,
        )(pos, early, late)

    def rounds(piece):
        got, both = [piece], []
        for k in range(1, 5):
            give = got[-1]
            if k > 2:
                give = choose(4 - k, got[k - 2], got[k - 1])
            pair = partners[k - 1]
            step = [
                ((i * n + j) * 2 + l, (pair[i, j, l][0] * n + pair[i, j, l][1]) * 2 + pair[i, j, l][2])
                for i, j, l in spots
            ]
            got.append(lax.ppermute(give, ("c", "z", "x"), step))
            both.append((got[k], swap("c", got[k])))
        return both

    own_tokens = latents.reshape(-1, model)
    count = own_tokens.shape[0]
    other_tokens = swap("y", own_tokens)
    far_live = swap("y", frames_live)
    group, plain, old = whole_call(
        functools.partial(table_kernel, heads, rows),
        [
            jax.ShapeDtypeStruct((width, heads * LANES), BF16),
            jax.ShapeDtypeStruct((width, heads * LANES), BF16),
            jax.ShapeDtypeStruct((units, rows, LANES), F32),
        ],
        "svv",
        0,
        2_000_000,
    )(pos, state_in.reshape(units, share, size), ksum_in.reshape(units, size))
    lead_blocks, tail_blocks = whole_call(
        block_kernel,
        [
            jax.ShapeDtypeStruct((members, 2 * count, rows_of), BF16)
            for rows_of in (half, depth - half)
        ],
        "svv",
        0,
        4_000_000,
    )(pos, own_tokens, other_tokens)

    def multiply(slots, split, acc, *given):
        first = [] if acc is None else [acc]
        wide = given[0].shape[-1]
        return whole_call(
            functools.partial(mul_kernel, slots, split, acc is None),
            jax.ShapeDtypeStruct((2 * count, wide), F32),
            "svv" + "v" * (len(first) + len(given)),
            1_500_000_000,
            5_000_000,
            alias={3: 0} if first else None,
        )(pos, lead_blocks, tail_blocks, *first, *given)

    if fast:
        kvs = [
            (a, e, a_there, e_there)
            for (a, a_there), (e, e_there) in zip(rounds(leads), rounds(tails))
        ]
        qs = rounds(wholes)
        acc = multiply((7, 8, 9), True, None, leads, tails, *kvs[0])
        acc = multiply((10, 11), True, acc, *kvs[1])
        acc = multiply((12, 13), True, acc, *kvs[2])
        asked = multiply((7, 8, 9, 10, 11), False, None, wholes, *qs[0], *qs[1])
        asked = multiply((12, 13), False, asked, *qs[2])
        last, last_kv, last_q = ("core",), kvs[3], qs[3]
    else:
        last = ("all",)
        whole_kv = [lax.all_gather(v, ("z", "x"), axis=0, tiled=False) for v in (leads, tails)]
        last_kv, last_q = whole_kv, [lax.all_gather(wholes, ("z", "x"), axis=0, tiled=False)]
        acc, asked = (jnp.zeros((2 * count, wide), F32) for wide in (wide_kv, wide_q))

    pairs = 2 * streams * heads
    chunk = jax.ShapeDtypeStruct((pairs, rows, LANES), BF16)
    parts = whole_call(
        functools.partial(kv_kernel, last, streams, frames, heads, size, rows),
        [chunk] * members,
        "sss" + "v" * (5 + len(last_kv)),
        1_500_000_000,
        5_000_000,
        scratch=[pltpu.VMEM(acc.shape, F32)],
    )(pos, frames_live, far_live, lead_blocks, tail_blocks, acc, *last_kv, group, plain)
    parts = list(parts)
    q, q_give = whole_call(
        functools.partial(ask_kernel, last, width),
        [
            jax.ShapeDtypeStruct((count, heads * LANES), BF16),
            jax.ShapeDtypeStruct((count, width), BF16),
        ],
        "svvvv" + "v" * len(last_q),
        700_000_000,
        3_000_000,
        scratch=[pltpu.VMEM(asked.shape, F32)],
    )(pos, lead_blocks, tail_blocks, asked, group, *last_q)

    far = members - 1
    parts[far - 1] = whole_call(
        add_kernel, chunk, "svv", 0, 250_000
    )(pos, parts[far - 1], xor(1, parts.pop()))
    for k in range(far - 1, 0, -1):
        parts[k] = xor(k, parts[k])
    q_other = swap("y", q_give)

    keep, give = whole_call(
        sum_kernel,
        [
            jax.ShapeDtypeStruct((pairs // 2, rows, LANES), F32),
            jax.ShapeDtypeStruct((pairs // 2, rows, LANES), BF16),
        ],
        "s" + "v" * far,
        0,
        1_000_000,
    )(pos, *parts)
    got = swap("y", give)
    new = whole_call(
        functools.partial(join_kernel, heads),
        jax.ShapeDtypeStruct((units, rows, LANES), BF16),
        "svvv",
        0,
        500_000,
    )(pos, keep, got, old)

    gathered = [new] + [xor(k, new) for k in range(1, far)]
    gathered.append(xor(1, gathered[far - 1]))
    q_other = whole_call(
        query_kernel,
        jax.ShapeDtypeStruct((count, heads * LANES), BF16),
        "svv",
        140_000_000,
        1_500_000,
    )(pos, q_other, group)

    every, spots, bit = [new], [0], owners // 2
    while bit:
        step = [(i, i ^ bit) for i in range(owners)]
        for i in range(len(every)):
            moved = lax.ppermute(every[i], ("o", "y", "c"), step)
            every.append(moved)
            spots.append(spots[i] ^ bit)
        bit //= 2
    place = whole_call(
        functools.partial(place_kernel, units),
        jax.ShapeDtypeStruct((units,), jnp.int32),
        "ss",
        0,
        1_000,
        smem=True,
    )(pos, new_place)
    moved_state, moved_ksum = whole_call(
        functools.partial(pick_kernel, share, size, rows, spots),
        [
            jax.ShapeDtypeStruct((units, share, size), F32),
            jax.ShapeDtypeStruct((units, size), F32),
        ],
        "s" + "v" * owners,
        1_000_000,
        800_000,
        scratch=[pltpu.VMEM((owners * units, rows, LANES), BF16)],
    )(place, *every)

    attended = whole_call(
        functools.partial(read_kernel, streams, frames, heads, size),
        jax.ShapeDtypeStruct((count, 2 * width), BF16),
        "ssvv" + "v" * members,
        1_500_000_000,
        3_000_000,
    )(pos, frames_live, q, q_other, *gathered)
    return (
        attended.reshape(streams, frames, spatial, 2 * width),
        moved_state,
        moved_ksum,
    )


def solution(mesh):
    owners, members = mesh.shape["req"], mesh.shape["mp"]
    split = Mesh(
        mesh.devices.reshape(owners // 4, 2, 2, members // 2, 2), ("o", "y", "c", "z", "x")
    )
    req, mp = ("o", "y", "c"), ("z", "x")
    return jax.shard_map(
        functools.partial(body, members // 2),
        mesh=split,
        in_specs=(
            P(req, None, mp, None),
            P(mp, None),
            P(req, None, mp, None),
            P(req, None, None),
            P(req),
            P(),
        ),
        out_specs=(P(req, None, mp, None), P(req, mp, None), P(req, None)),
        check_vma=False,
    )
```
